128 devices in a mesh: det: 4 (over x), tm: 32 (over y, z, core).
Axes of the slice: x: 4, y: 4, z: 4, core: 2. Of those that a mesh axis runs over, the one named last changes fastest.
Arguments:
- tod: bfloat16 [8, 2048, 256], P('det', 'tm'), may hold values from -6 to 6
- pointing: bfloat16 [8, 2048, 256, 128], P('det', 'tm'), may hold values from -0.5 to 0.5
- weights: float32 [8, 2048, 256], P('det', 'tm'), may hold values from 0.2 to 2
- tile_ids: int32 [8, 2048], P('det', 'tm'), may hold values from 0 to 2047, as said below
- offsets: int32 [8, 2048], P('det', 'tm'), may hold values from 0 to 896
- neighbours: int32 [2048, 2], P(('det', 'tm')), may hold values from 0 to 2047, as said below
Outputs:
- solution: float32 [2048, 1024], P(('det', 'tm'))
- residual: float32 [2048, 1024], P(('det', 'tm'))
The draws below stay inside these ranges and needn't reach their ends.
Inputs may be any that keep to these rules, and one draw needn't show every extreme that they name: `tile_ids`: take the blocks of one device (detectors of one index of det, time blocks of one index of tm) in detector-major order: each consecutive run of 2 of them names tiles of one owner device (tile // 16), different runs name different owners, so at most 2 blocks of one device name one owner, and this is reached; some owner is named by 2 blocks of every device. The tiles form one cycle: neighbours[neighbours[t,1],0] == t for every tile t.
All inputs are finite; a program needn't handle non-finite values.
Results may differ from the reference program's by a relative error of at most 0.017.
Values may be sent and summed in bfloat16 or wider, within the bound.
No kernel may reach another device: no remote copies, remote signals or barrier semaphores. Data moves between devices by JAX's collectives and lax.ppermute only.
A program may use at most 64 MiB of HBM per device.

```python
import math
import jax
import jax.numpy as jnp
from jax import lax

SAMP = 256
FOOT = 128
TILE_PIX = 1024
ITERS = 2
DET_DEV = 2
TB_DEV = 64
TILE_DEV = 16
CAP = 2
NDET = 8
NTB = 2048
TILES = 2048
N_TM = 32
DEVICES = 128


def draw_tile_ids(key, part):
    group_count = DET_DEV * TB_DEV // CAP
    key_pop, key_noise, key_slot = jax.random.split(key, 3)
    frequent_pixels = jax.random.randint(key_pop, (), 0, DEVICES)
    noise_lookup_table = jax.random.randint(key_noise, (DEVICES, DEVICES), 0, 65536)
    column_list = jnp.arange(DEVICES, dtype=jnp.int32)
    extra_reward = jnp.where(column_list == frequent_pixels, 1 << 24, 0).astype(jnp.int32)
    score_values = noise_lookup_table * DEVICES + column_list[None, :] + extra_reward[None, :]
    unused, destinations = lax.top_k(score_values, group_count)
    det_index = jnp.arange(NDET, dtype=jnp.int32)[:, None]
    time_index = jnp.arange(NTB, dtype=jnp.int32)[None, :]
    source = det_index // DET_DEV * N_TM + time_index // TB_DEV
    local_pos = det_index % DET_DEV * TB_DEV + time_index % TB_DEV
    owner_dev = destinations[source, local_pos // CAP]
    slot_tile = jax.random.randint(key_slot, (NDET, NTB), 0, TILE_DEV)
    return (owner_dev * TILE_DEV + slot_tile).astype(jnp.int32)


def draw_offsets(key, part):
    key_kind, key_pos = jax.random.split(jax.random.fold_in(key, 7), 2)
    kind_pick = jax.random.randint(key_kind, (NDET, NTB), 0, 4)
    spread_pos = jax.random.randint(key_pos, (NDET, NTB), 0, TILE_PIX - FOOT + 1)
    ends_pos = jnp.where(kind_pick == 0, 0, TILE_PIX - FOOT)
    first_set = jnp.zeros((NDET, NTB), jnp.int32).at[0, 0].set(1).at[0, 1].set(2)
    kind_pick = jnp.where(first_set == 1, 0, jnp.where(first_set == 2, 1, kind_pick))
    return jnp.where(kind_pick <= 1, ends_pos, spread_pos).astype(jnp.int32)


def draw_neighbours(key, part):
    order_loop = jax.random.permutation(key, TILES).astype(jnp.int32)
    after_loop = jnp.roll(order_loop, -1)
    before_loop = jnp.roll(order_loop, 1)
    next_tile = jnp.zeros((TILES,), jnp.int32).at[order_loop].set(after_loop)
    prev_tile = jnp.zeros((TILES,), jnp.int32).at[order_loop].set(before_loop)
    return jnp.stack([prev_tile, next_tile], axis=1).astype(jnp.int32)


def level_of(rng, shape, pieces, smallest, high):
    factor_of, own = 1.0, jax.random.fold_in(rng, 6)
    for position, blocks in pieces:
        heights = jnp.exp(jax.random.uniform(jax.random.fold_in(own, position), (blocks,), jnp.float32, smallest / len(pieces), high / len(pieces)))
        factor_of = factor_of * jnp.repeat(heights, shape[position] // blocks).reshape([-1 if axis == position else 1 for axis in range(len(shape))])
    return factor_of


def centred(stream_key, dims, scale, reach, cuts=(), kind=jnp.bfloat16):
    factor_of = level_of(stream_key, dims, cuts, -0.22, 0.18) if cuts else 1.0
    array = jax.random.normal(stream_key, dims, jnp.float32) * scale * factor_of
    return jnp.minimum(jnp.maximum(array, -reach), reach).astype(kind)


def setup_inputs(seed: int = 0) -> dict:
    splits = jax.random.split(jax.random.key(seed), 7)
    return {
        "tod": centred(splits[0], (NDET, NTB, SAMP), 1.0, 6.0, ((0, 4), (1, 32))),
        "pointing": centred(splits[1], (NDET, NTB, SAMP, FOOT), FOOT ** -0.5, 0.5, ((0, 4), (1, 32))),
        "weights": jnp.clip(jnp.exp(math.log(2.0) - 2.3025851 * jax.random.uniform(splits[2], (NDET, NTB, SAMP), jnp.float32) ** level_of(splits[2], (NDET, NTB, SAMP), ((0, 4), (1, 32)), -0.2, 0.2)), 0.2, 2.0),
        "tile_ids": draw_tile_ids(jax.random.fold_in(splits[6], 71), 0),
        "offsets": draw_offsets(jax.random.fold_in(splits[6], 71), 0),
        "neighbours": draw_neighbours(jax.random.fold_in(splits[6], 71), 0),
    }


smooth_weight = 2.0
ridge_weight = 0.5


def prior_term(map_field, neighbours):
    left_edge = map_field[neighbours[:, 0], TILE_PIX - 1]
    right_edge = map_field[neighbours[:, 1], 0]
    lefts = jnp.concatenate([left_edge[:, None], map_field[:, :-1]], axis=1)
    rights = jnp.concatenate([map_field[:, 1:], right_edge[:, None]], axis=1)
    return smooth_weight * (2.0 * map_field - lefts - rights) + ridge_weight * map_field


def to_bf16_and_back(values):
    return lax.optimization_barrier(values.astype(jnp.bfloat16)).astype(jnp.float32)


def reference(tod, pointing, weights, tile_ids, offsets, neighbours):
    foot_range = jnp.arange(FOOT, dtype=jnp.int32)
    first_pixel_index = (tile_ids * TILE_PIX + offsets).astype(jnp.int32)

    def accumulate(back_vals):
        index_all = (first_pixel_index[:, :, None] + foot_range).reshape(-1)
        total = jnp.zeros((TILES * TILE_PIX,), jnp.float32).at[index_all].add(back_vals.reshape(-1))
        return total.reshape(TILES, TILE_PIX)

    def apply_normal(map_field):
        flat_map = map_field.reshape(-1)

        def one_row(row_items):
            beam_row, weight_row, start_row = row_items
            beam_wide = beam_row.astype(jnp.float32)
            foot = to_bf16_and_back(flat_map[start_row[:, None] + foot_range])
            samples = jnp.einsum('tsf,tf->ts', beam_wide, foot, precision=lax.Precision.HIGHEST)
            weighted = to_bf16_and_back(weight_row * samples)
            return jnp.einsum('tsf,ts->tf', beam_wide, weighted, precision=lax.Precision.HIGHEST)

        back_vals = lax.map(one_row, (pointing, weights, first_pixel_index))
        return accumulate(back_vals) + prior_term(map_field, neighbours)

    def rhs_row(row_items):
        beam_row, weight_row, tod_row = row_items
        weighted = to_bf16_and_back(weight_row * tod_row.astype(jnp.float32))
        return jnp.einsum('tsf,ts->tf', beam_row.astype(jnp.float32), weighted, precision=lax.Precision.HIGHEST)

    right_hand_vector = accumulate(lax.map(rhs_row, (pointing, weights, tod)))
    solution = jnp.zeros_like(right_hand_vector)
    residual = right_hand_vector
    direction = right_hand_vector
    norm_now = jnp.sum(residual * residual)
    for iteration in range(ITERS):
        image_vec = apply_normal(direction)
        step_size = norm_now / jnp.sum(direction * image_vec)
        solution = solution + step_size * direction
        residual = residual - step_size * image_vec
        norm_next = jnp.sum(residual * residual)
        direction = residual + (norm_next / norm_now) * direction
        norm_now = norm_next
    return solution, residual
```

```python
import jax
import jax.numpy as jnp
from jax import lax
from jax.experimental import pallas as pl
from jax.experimental.pallas import tpu as pltpu
from jax.sharding import Mesh
from jax.sharding import PartitionSpec as P


DET_TM = ("det", "tm_0", "tm_1", "tm_2")
TM = ("tm_0", "tm_1", "tm_2")
SAMP = 256
FOOT = 128
L = 128
TILE = 16
ROW_STEP = 16
SCALARS = 64

smooth_weight = 2.0
ridge_weight = 0.5

F32 = jnp.float32
BF16 = jnp.bfloat16


def _roll(x, shift, axis):
    return pltpu.roll(x, shift, axis)


def _iota(shape, dim):
    return lax.broadcasted_iota(jnp.int32, shape, dim)


def _dot(a, b):
    return jnp.dot(a, b, preferred_element_type=F32)


def _dot_nt(a, b):
    return lax.dot_general(a, b, (((1,), (1,)), ((), ())), preferred_element_type=F32)


def _onehot(mask):
    return jnp.where(mask, 1.0, 0.0).astype(BF16)


def _to_col(row):
    eye = _iota((L, L), 0) == _iota((L, L), 1)
    return jnp.sum(jnp.where(eye, row, 0.0), axis=1, keepdims=True)


def _to_row(col):
    eye = _iota((L, L), 0) == _iota((L, L), 1)
    return jnp.sum(jnp.where(eye, col, 0.0), axis=0, keepdims=True)


def _rotate(x, amount):
    for bit in range(7):
        x = jnp.where((amount & (1 << bit)) != 0, _roll(x, 1 << bit, 1), x)
    return x


def _as_row(ids, scratch):
    scratch[...] = jnp.zeros(scratch.shape, F32)
    scratch[0:2, 0:64] = ids.astype(F32)
    x = scratch[...]
    return x[0:1] + _roll(x, 64, 1)[1:2]


def _pieces(value, first):
    hi = value.astype(BF16).astype(F32)
    mid = (value - hi).astype(BF16).astype(F32)
    lo = value - hi - mid
    lane = _iota((1, L), 1)
    return jnp.where(
        lane == first, hi, jnp.where(lane == first + 1, mid, jnp.where(lane == first + 2, lo, 0.0))
    )


def _whole(row, first):
    lane = _iota((1, L), 1)
    return jnp.sum(
        jnp.where((lane >= first) & (lane < first + 3), row, 0.0), axis=1, keepdims=True
    )


def _total(x):
    return jnp.sum(jnp.sum(x, axis=0, keepdims=True), axis=1, keepdims=True)


def _blocks_of(owner_row, j):
    block = _iota((L, L), 1)
    return _onehot((_iota((L, L), 0) == owner_row) & ((block & 1) == j))


def first_message(tile_row, offset_row, back):
    tile = tile_row.astype(jnp.int32)
    offset = offset_row.astype(jnp.int32)
    owner = tile >> 4
    start_row = (offset >> 7) * ROW_STEP + (tile & 15)
    shift = offset & 127
    shift_col = _to_col(shift.astype(F32)).astype(jnp.int32)
    turned = _rotate(back, shift_col).astype(BF16)
    to_0 = _blocks_of(owner, 0)
    to_1 = _blocks_of(owner, 1)
    line = _iota((L, L), 0)
    place = 2 * (_iota((L, L), 1) & 1)
    facts = jnp.where(
        line == place,
        start_row.astype(F32),
        jnp.where(line == place + 1, shift.astype(F32), 0.0),
    ).astype(BF16)
    return (
        _dot(to_0, turned).astype(BF16),
        _dot(to_1, turned).astype(BF16),
        _dot_nt(to_0 + to_1, facts).astype(BF16),
    )


def block_tables(tile_row, offset_row):
    owner = tile_row.astype(jnp.int32) >> 4
    shift = offset_row.astype(jnp.int32) & 127
    owner_col = _to_col(owner.astype(F32)).astype(jnp.int32)
    shift_col = _to_col(shift.astype(F32)).astype(jnp.int32)
    block = _iota((L, L), 0)
    device = _iota((L, L), 1)
    get = [_onehot((device == owner_col) & ((block & 1) == j)) for j in range(2)]
    put = [_blocks_of(owner, j) for j in range(2)]
    return get, put, jnp.broadcast_to(shift_col, (L, L))


def owner_tables(facts):
    facts = facts.astype(F32)
    pick, place, shifts = [], [], []
    for j in range(2):
        start_col = facts[:, 2 * j : 2 * j + 1]
        start_row = _to_row(start_col)
        for step in (0, ROW_STEP):
            pick.append(_onehot(_iota((L, L), 1).astype(F32) == start_col + step))
            place.append(_onehot(_iota((L, L), 0).astype(F32) == start_row + step))
        shifts.append(jnp.broadcast_to(facts[:, 2 * j + 1 : 2 * j + 2], (L, L)).astype(jnp.int32))
    return pick, place, shifts


def add_up(got, place, shifts):
    lane = _iota((L, L), 1)
    total = None
    for j in range(2):
        x = got[j].astype(F32)
        upper = jnp.where(lane >= shifts[j], x, 0.0).astype(BF16)
        lower = jnp.where(lane < shifts[j], x, 0.0).astype(BF16)
        part = _dot(place[2 * j], upper) + _dot(place[2 * j + 1], lower)
        total = part if total is None else total + part
    return total


def reply(field, pick, shifts):
    lane = _iota((L, L), 1)
    field = field.astype(BF16)
    return [
        jnp.where(
            lane >= shifts[j], _dot(pick[2 * j], field), _dot(pick[2 * j + 1], field)
        ).astype(BF16)
        for j in range(2)
    ]


def edge_row(field):
    lane = _iota((TILE, L), 1)
    tile = _iota((TILE, L), 0)
    first = field[0:TILE, 0:1]
    last = field[L - TILE : L, L - 1 : L]
    out = jnp.zeros((TILE, L), F32)
    for k, value in enumerate((first, last)):
        hi = value.astype(BF16).astype(F32)
        out = out + jnp.where(lane == tile + 32 * k, hi, 0.0)
        out = out + jnp.where(lane == tile + 32 * k + 16, value - hi, 0.0)
    return jnp.sum(out, axis=0, keepdims=True)


def outer_edges(edges, neighbours):
    lane = _iota((TILE, L), 1)
    found = []
    for side, base in ((0, 32), (1, 0)):
        tile = neighbours[:, side : side + 1]
        rows = _dot(_onehot(lane == (tile >> 4)), edges)
        at = base + (tile & 15)
        found.append(
            jnp.sum(jnp.where((lane == at) | (lane == at + 16), rows, 0.0), axis=1, keepdims=True)
        )
    return found


def prior(field, before, after):
    lane = _iota((L, L), 1)
    row = _iota((L, L), 0)
    to_right = _roll(field, 1, 1)
    to_left = _roll(field, L - 1, 1)
    left_in = _roll(to_right, ROW_STEP, 0)
    right_in = _roll(to_left, L - ROW_STEP, 0)
    pad = jnp.zeros((L - TILE, 1), F32)
    left_in = jnp.where(row < TILE, jnp.concatenate([before, pad], axis=0), left_in)
    right_in = jnp.where(row >= L - TILE, jnp.concatenate([pad, after], axis=0), right_in)
    lefts = jnp.where(lane == 0, left_in, to_right)
    rights = jnp.where(lane == L - 1, right_in, to_left)
    return smooth_weight * (2.0 * field - lefts - rights) + ridge_weight * field


def take_reply(got, get, shift):
    turned = _dot(get[0], got[0]) + _dot(get[1], got[1])
    return _rotate(turned, (L - shift) & 127)


def send_back(back, put, shift):
    turned = _rotate(back, shift).astype(BF16)
    return [_dot(put[j], turned).astype(BF16) for j in range(2)]


def pair_rows(foot):
    row = _iota((L, L), 0)
    left = jnp.where(row < L // 2, foot, 0.0).astype(BF16)
    right = jnp.where(row >= L // 2, foot, 0.0).astype(BF16)
    return jnp.concatenate([left, right], axis=1)


RHS_STEP = 16
NORMAL_STEP = 8
APPLY_STEP = 16


def rhs_kernel(tile_ref, offset_ref, tod_ref, weight_ref, beam_ref, message_ref, back, scratch):
    g = pl.program_id(0)
    weighted = (weight_ref[...] * tod_ref[...].astype(F32)).astype(BF16)
    row = _iota((RHS_STEP, FOOT), 0)
    out = jnp.zeros((RHS_STEP, FOOT), F32)
    for k in range(RHS_STEP):
        out = jnp.where(row == k, _dot(weighted, beam_ref[k]), out)
    back[pl.ds(pl.multiple_of(g * RHS_STEP, RHS_STEP), RHS_STEP), :] = out

    @pl.when(g == pl.num_programs(0) - 1)
    def _():
        tile_row = _as_row(tile_ref[...], scratch)
        offset_row = _as_row(offset_ref[...], scratch)
        parts = first_message(tile_row, offset_row, back[...])
        for k in range(3):
            message_ref[k] = parts[k]


def normal_kernel(tile_ref, offset_ref, weight_ref, beam_ref, normal_ref, get_ref, put_ref, shift_ref, scratch):
    for k in range(NORMAL_STEP):
        for det in range(2):
            beam = beam_ref[det, k]
            turned = beam.astype(F32).T * weight_ref[det, k : k + 1, :]
            normal_ref[k, :, det * FOOT : (det + 1) * FOOT] = _dot(turned.astype(BF16), beam).astype(BF16)

    @pl.when(pl.program_id(0) == 0)
    def _():
        tile_row = _as_row(tile_ref[...], scratch)
        offset_row = _as_row(offset_ref[...], scratch)
        get, put, shift = block_tables(tile_row, offset_row)
        for j in range(2):
            get_ref[j] = get[j]
            put_ref[j] = put[j]
        shift_ref[...] = shift


def start_kernel(got_ref, field_ref, message_ref, pick_ref, place_ref, shift_ref):
    pick, place, shifts = owner_tables(got_ref[2])
    field = add_up((got_ref[0], got_ref[1]), place, shifts)
    replies = reply(field, pick, shifts)
    field_ref[...] = field
    message_ref[0] = replies[0]
    message_ref[1] = replies[1]
    message_ref[2] = jnp.broadcast_to(edge_row(field), (L, L)).astype(BF16)
    for k in range(4):
        pick_ref[k] = pick[k]
        place_ref[k] = place[k]
    for j in range(2):
        shift_ref[j] = shifts[j]


def apply_step(normal_ref, pairs, back):
    g = pl.program_id(0)
    lane = _iota((L, L), 1) & 63
    out = _dot_nt(normal_ref[...].reshape(APPLY_STEP * L, 2 * L), pairs[...])
    acc = back[...]
    for k in range(APPLY_STEP):
        acc = jnp.where(lane == g * APPLY_STEP + k, out[k * L : (k + 1) * L], acc)
    back[...] = acc


def first_apply_kernel(got_ref, get_ref, put_ref, shift_ref, normal_ref, message_ref, foot_ref, pairs, back):
    g = pl.program_id(0)

    @pl.when(g == 0)
    def _():
        foot = take_reply((got_ref[0], got_ref[1]), (get_ref[0], get_ref[1]), shift_ref[...])
        foot_ref[...] = foot
        pairs[...] = pair_rows(foot)
        back[...] = jnp.zeros((L, L), F32)

    apply_step(normal_ref, pairs, back)

    @pl.when(g == pl.num_programs(0) - 1)
    def _():
        parts = send_back(back[...].T, (put_ref[0], put_ref[1]), shift_ref[...])
        message_ref[0] = parts[0]
        message_ref[1] = parts[1]


def middle_kernel(got_ref, before_ref, field_ref, neighbour_ref, pick_ref, place_ref, shift_ref, image_ref, prior_ref, message_ref):
    field = field_ref[...]
    pick = [pick_ref[k] for k in range(4)]
    place = [place_ref[k] for k in range(4)]
    shifts = [shift_ref[j] for j in range(2)]
    before, after = outer_edges(before_ref[2], neighbour_ref[...])
    smooth = prior(field, before, after)
    image = add_up((got_ref[0], got_ref[1]), place, shifts) + smooth
    replies = reply(image, pick, shifts)
    prior_ref[...] = smooth
    image_ref[...] = image
    message_ref[0] = replies[0]
    message_ref[1] = replies[1]
    extra = (
        edge_row(image)
        + _pieces(_total(field * field), SCALARS)
        + _pieces(_total(field * image), SCALARS + 3)
    )
    message_ref[2] = jnp.broadcast_to(extra, (L, L)).astype(BF16)


def second_apply_kernel(
    got_ref, get_ref, put_ref, shift_ref, normal_ref, foot_ref, field_ref, image_ref, smooth_ref, neighbour_ref,
    message_ref, residual_ref, prior_ref, sums_ref, pairs, back, foot_scr,
):
    g = pl.program_id(0)

    @pl.when(g == 0)
    def _():
        sums = jnp.sum(got_ref[2].astype(F32), axis=0, keepdims=True)
        sums_ref[...] = sums
        step = _whole(sums, SCALARS) / _whole(sums, SCALARS + 3)
        taken = take_reply((got_ref[0], got_ref[1]), (get_ref[0], get_ref[1]), shift_ref[...])
        foot = (foot_ref[...] - step * taken).astype(BF16).astype(F32)
        foot_scr[...] = foot
        pairs[...] = pair_rows(foot)
        back[...] = jnp.zeros((L, L), F32)
        image = image_ref[...]
        before, after = outer_edges(got_ref[2], neighbour_ref[...])
        residual_ref[...] = field_ref[...] - step * image
        prior_ref[...] = smooth_ref[...] - step * prior(image, before, after)

    apply_step(normal_ref, pairs, back)

    @pl.when(g == pl.num_programs(0) - 1)
    def _():
        turned = back[...].T
        parts = send_back(turned, (put_ref[0], put_ref[1]), shift_ref[...])
        message_ref[0] = parts[0]
        message_ref[1] = parts[1]
        residual = residual_ref[...]
        square = _total(residual * residual)
        product = _total(foot_scr[...] * turned + residual * prior_ref[...])
        extra = _pieces(square, SCALARS) + _pieces(product, SCALARS + 3)
        message_ref[2] = jnp.broadcast_to(extra, (L, L)).astype(BF16)


def last_kernel(got_ref, place_ref, shift_ref, field_ref, image_ref, residual_ref, smooth_ref, sums_ref, solution_ref, rest_ref):
    place = [place_ref[k] for k in range(4)]
    shifts = [shift_ref[j] for j in range(2)]
    residual = residual_ref[...]
    field = field_ref[...]
    image = add_up((got_ref[0], got_ref[1]), place, shifts) + smooth_ref[...]
    sums = sums_ref[...]
    more = jnp.sum(got_ref[2].astype(F32), axis=0, keepdims=True)
    norm_first = _whole(sums, SCALARS)
    step_first = norm_first / _whole(sums, SCALARS + 3)
    norm = _whole(more, SCALARS)
    ratio = norm / norm_first
    step = norm / (_whole(more, SCALARS + 3) - ratio * norm / step_first)
    solution = step_first * field + step * (residual + ratio * field)
    rest = residual - step * (image + ratio * image_ref[...])
    for q in range(8):
        solution_ref[:, q * L : (q + 1) * L] = solution[q * TILE : (q + 1) * TILE]
        rest_ref[:, q * L : (q + 1) * L] = rest[q * TILE : (q + 1) * TILE]


def _shape(shape, dtype):
    return jax.ShapeDtypeStruct(shape, dtype)


def _full(shape):
    return pl.BlockSpec(shape, lambda g: (0,) * len(shape))


MAP = (L, L)
WIDE = _shape(MAP, F32)


def call(kernel, grid, in_specs, outs, out_specs, scratch, args, flops, size):
    return pl.pallas_call(
        kernel,
        grid=(grid,),
        in_specs=in_specs,
        out_specs=out_specs,
        out_shape=outs,
        scratch_shapes=scratch,
        compiler_params=pltpu.CompilerParams(
            dimension_semantics=("arbitrary",), vmem_limit_bytes=40 * 2**20
        ),
        cost_estimate=pl.CostEstimate(flops=flops, bytes_accessed=size, transcendentals=0),
    )(*args)


def whole_call(kernel, outs, args, scratch=()):
    return call(
        kernel, 1, [_full(a.shape) for a in args], outs, [_full(o.shape) for o in outs], scratch, args, 2**25, 2**19
    )


def exchange(x):
    return lax.all_to_all(x, DET_TM, split_axis=1, concat_axis=1, tiled=True)


def per_device(tod, pointing, weights, tile_ids, offsets, neighbours):
    ids = [_full(tile_ids.shape)] * 2
    half = L // 2

    (message,) = call(
        rhs_kernel,
        L // RHS_STEP,
        ids
        + [
            pl.BlockSpec((RHS_STEP, SAMP), lambda g: (g, 0)),
            pl.BlockSpec((RHS_STEP, SAMP), lambda g: (g, 0)),
            pl.BlockSpec((RHS_STEP, SAMP, FOOT), lambda g: (g, 0, 0)),
        ],
        [_shape((3, L, L), BF16)],
        [_full((3, L, L))],
        [pltpu.VMEM((L, FOOT), F32), pltpu.VMEM((8, L), F32)],
        (
            tile_ids,
            offsets,
            tod.reshape(L, SAMP),
            weights.reshape(L, SAMP),
            pointing.reshape(L, SAMP, FOOT),
        ),
        2**24,
        2**23,
    )
    got = exchange(message)

    normal, get, put, shift = call(
        normal_kernel,
        half // NORMAL_STEP,
        ids
        + [
            pl.BlockSpec((2, NORMAL_STEP, SAMP), lambda g: (0, g, 0)),
            pl.BlockSpec((2, NORMAL_STEP, SAMP, FOOT), lambda g: (0, g, 0, 0)),
        ],
        [
            _shape((half, FOOT, 2 * FOOT), BF16),
            _shape((2, L, L), BF16),
            _shape((2, L, L), BF16),
            _shape((L, L), jnp.int32),
        ],
        [
            pl.BlockSpec((NORMAL_STEP, FOOT, 2 * FOOT), lambda g: (g, 0, 0)),
            _full((2, L, L)),
            _full((2, L, L)),
            _full((L, L)),
        ],
        [pltpu.VMEM((8, L), F32)],
        (tile_ids, offsets, weights, pointing),
        2**30,
        12 * 2**20,
    )

    field, message, pick, place, shifts = whole_call(
        start_kernel,
        [WIDE, _shape((3, L, L), BF16), _shape((4, L, L), BF16), _shape((4, L, L), BF16), _shape((2, L, L), jnp.int32)],
        (got,),
    )
    got_first = exchange(message)

    normal_spec = pl.BlockSpec((APPLY_STEP, FOOT, 2 * FOOT), lambda g: (g, 0, 0))
    table_specs = [_full((2, L, L)), _full((2, L, L)), _full((L, L)), normal_spec]
    message, foot = call(
        first_apply_kernel,
        half // APPLY_STEP,
        [_full((3, L, L))] + table_specs,
        [_shape((2, L, L), BF16), WIDE],
        [_full((2, L, L)), _full(MAP)],
        [pltpu.VMEM((L, 2 * L), BF16), pltpu.VMEM(MAP, F32)],
        (got_first, get, put, shift, normal),
        2**29,
        2**22,
    )
    got = exchange(message)

    image, smooth, message = whole_call(
        middle_kernel,
        [WIDE, WIDE, _shape((3, L, L), BF16)],
        (got, got_first, field, neighbours, pick, place, shifts),
    )
    got = exchange(message)

    message, residual, smooth, sums = call(
        second_apply_kernel,
        half // APPLY_STEP,
        [_full((3, L, L))] + table_specs + [_full(MAP)] * 4 + [_full(neighbours.shape)],
        [_shape((3, L, L), BF16), WIDE, WIDE, _shape((1, L), F32)],
        [_full((3, L, L)), _full(MAP), _full(MAP), _full((1, L))],
        [pltpu.VMEM((L, 2 * L), BF16), pltpu.VMEM(MAP, F32), pltpu.VMEM(MAP, F32)],
        (got, get, put, shift, normal, foot, field, image, smooth, neighbours),
        2**29,
        2**22,
    )
    got = exchange(message)

    return tuple(
        whole_call(
            last_kernel,
            [_shape((TILE, 8 * L), F32)] * 2,
            (got, place, shifts, field, image, residual, smooth, sums),
        )
    )


def solution(mesh):
    split = Mesh(mesh.devices.reshape(mesh.shape["det"], 4, 4, 2), DET_TM)
    in_specs = (
        P("det", TM, None),
        P("det", TM, None, None),
        P("det", TM, None),
        P("det", TM),
        P("det", TM),
        P(DET_TM, None),
    )
    out_specs = (P(DET_TM, None), P(DET_TM, None))
    return jax.shard_map(
        per_device, mesh=split, in_specs=in_specs, out_specs=out_specs, check_vma=False
    )
```

```python
import jax
import jax.numpy as jnp
from jax import lax
from jax.experimental import pallas as pl
from jax.experimental.pallas import tpu as pltpu
from jax.sharding import Mesh
from jax.sharding import PartitionSpec as P


DET_TM = ("det", "tm_0", "tm_1", "tm_2")
TM = ("tm_0", "tm_1", "tm_2")
SAMP = 256
FOOT = 128
L = 128
TILE = 16
ROW_STEP = 16
SCALARS = 64

smooth_weight = 2.0
ridge_weight = 0.5

F32 = jnp.float32
BF16 = jnp.bfloat16


def _roll(x, shift, axis):
    return pltpu.roll(x, shift, axis)


def _iota(shape, dim):
    return lax.broadcasted_iota(jnp.int32, shape, dim)


def _dot(a, b):
    return jnp.dot(a, b, preferred_element_type=F32)


def _dot_nt(a, b):
    return lax.dot_general(a, b, (((1,), (1,)), ((), ())), preferred_element_type=F32)


def _onehot(mask):
    return jnp.where(mask, 1.0, 0.0).astype(BF16)


def _to_col(row):
    eye = _iota((L, L), 0) == _iota((L, L), 1)
    return jnp.sum(jnp.where(eye, row, 0.0), axis=1, keepdims=True)


def _to_row(col):
    eye = _iota((L, L), 0) == _iota((L, L), 1)
    return jnp.sum(jnp.where(eye, col, 0.0), axis=0, keepdims=True)


def _rotate(x, amount):
    for bit in range(7):
        x = jnp.where((amount & (1 << bit)) != 0, _roll(x, 1 << bit, 1), x)
    return x


def _as_row(ids, scratch):
    scratch[...] = jnp.zeros(scratch.shape, F32)
    scratch[0:2, 0:64] = ids.astype(F32)
    x = scratch[...]
    return x[0:1] + _roll(x, 64, 1)[1:2]


def _pieces(value, first):
    hi = value.astype(BF16).astype(F32)
    mid = (value - hi).astype(BF16).astype(F32)
    lo = value - hi - mid
    lane = _iota((1, L), 1)
    return jnp.where(
        lane == first, hi, jnp.where(lane == first + 1, mid, jnp.where(lane == first + 2, lo, 0.0))
    )


def _whole(row, first):
    lane = _iota((1, L), 1)
    return jnp.sum(
        jnp.where((lane >= first) & (lane < first + 3), row, 0.0), axis=1, keepdims=True
    )


def _total(x):
    return jnp.sum(jnp.sum(x, axis=0, keepdims=True), axis=1, keepdims=True)


def _blocks_of(owner_row, j):
    block = _iota((L, L), 1)
    return _onehot((_iota((L, L), 0) == owner_row) & ((block & 1) == j))


def first_message(tile_row, offset_row, back):
    tile = tile_row.astype(jnp.int32)
    offset = offset_row.astype(jnp.int32)
    owner = tile >> 4
    start_row = (offset >> 7) * ROW_STEP + (tile & 15)
    shift = offset & 127
    shift_col = _to_col(shift.astype(F32)).astype(jnp.int32)
    turned = _rotate(back, shift_col).astype(BF16)
    to_0 = _blocks_of(owner, 0)
    to_1 = _blocks_of(owner, 1)
    line = _iota((L, L), 0)
    place = 2 * (_iota((L, L), 1) & 1)
    facts = jnp.where(
        line == place,
        start_row.astype(F32),
        jnp.where(line == place + 1, shift.astype(F32), 0.0),
    ).astype(BF16)
    return (
        _dot(to_0, turned).astype(BF16),
        _dot(to_1, turned).astype(BF16),
        _dot_nt(to_0 + to_1, facts).astype(BF16),
    )


def block_tables(tile_row, offset_row):
    owner = tile_row.astype(jnp.int32) >> 4
    shift = offset_row.astype(jnp.int32) & 127
    owner_col = _to_col(owner.astype(F32)).astype(jnp.int32)
    shift_col = _to_col(shift.astype(F32)).astype(jnp.int32)
    block = _iota((L, L), 0)
    device = _iota((L, L), 1)
    get = [_onehot((device == owner_col) & ((block & 1) == j)) for j in range(2)]
    put = [_blocks_of(owner, j) for j in range(2)]
    return get, put, jnp.broadcast_to(shift_col, (L, L))


def owner_tables(facts):
    facts = facts.astype(F32)
    pick, place, shifts = [], [], []
    for j in range(2):
        start_col = facts[:, 2 * j : 2 * j + 1]
        start_row = _to_row(start_col)
        for step in (0, ROW_STEP):
            pick.append(_onehot(_iota((L, L), 1).astype(F32) == start_col + step))
            place.append(_onehot(_iota((L, L), 0).astype(F32) == start_row + step))
        shifts.append(jnp.broadcast_to(facts[:, 2 * j + 1 : 2 * j + 2], (L, L)).astype(jnp.int32))
    return pick, place, shifts


def add_up(got, place, shifts):
    lane = _iota((L, L), 1)
    total = None
    for j in range(2):
        x = got[j].astype(F32)
        upper = jnp.where(lane >= shifts[j], x, 0.0).astype(BF16)
        lower = jnp.where(lane < shifts[j], x, 0.0).astype(BF16)
        part = _dot(place[2 * j], upper) + _dot(place[2 * j + 1], lower)
        total = part if total is None else total + part
    return total


def reply(field, pick, shifts):
    lane = _iota((L, L), 1)
    field = field.astype(BF16)
    return [
        jnp.where(
            lane >= shifts[j], _dot(pick[2 * j], field), _dot(pick[2 * j + 1], field)
        ).astype(BF16)
        for j in range(2)
    ]


def edge_row(field):
    lane = _iota((TILE, L), 1)
    tile = _iota((TILE, L), 0)
    first = field[0:TILE, 0:1]
    last = field[L - TILE : L, L - 1 : L]
    out = jnp.zeros((TILE, L), F32)
    for k, value in enumerate((first, last)):
        hi = value.astype(BF16).astype(F32)
        out = out + jnp.where(lane == tile + 32 * k, hi, 0.0)
        out = out + jnp.where(lane == tile + 32 * k + 16, value - hi, 0.0)
    return jnp.sum(out, axis=0, keepdims=True)


def outer_edges(edges, neighbours):
    lane = _iota((TILE, L), 1)
    found = []
    for side, base in ((0, 32), (1, 0)):
        line = neighbours[side : side + 1].astype(F32)
        own = _iota((TILE, TILE), 0) == _iota((TILE, TILE), 1)
        tile = jnp.sum(jnp.where(own, line, 0.0), axis=1, keepdims=True).astype(jnp.int32)
        rows = _dot(_onehot(lane == (tile >> 4)), edges)
        at = base + (tile & 15)
        found.append(
            jnp.sum(jnp.where((lane == at) | (lane == at + 16), rows, 0.0), axis=1, keepdims=True)
        )
    return found


def prior(field, before, after):
    lane = _iota((L, L), 1)
    row = _iota((L, L), 0)
    to_right = _roll(field, 1, 1)
    to_left = _roll(field, L - 1, 1)
    left_in = _roll(to_right, ROW_STEP, 0)
    right_in = _roll(to_left, L - ROW_STEP, 0)
    pad = jnp.zeros((L - TILE, 1), F32)
    left_in = jnp.where(row < TILE, jnp.concatenate([before, pad], axis=0), left_in)
    right_in = jnp.where(row >= L - TILE, jnp.concatenate([pad, after], axis=0), right_in)
    lefts = jnp.where(lane == 0, left_in, to_right)
    rights = jnp.where(lane == L - 1, right_in, to_left)
    return smooth_weight * (2.0 * field - lefts - rights) + ridge_weight * field


def take_reply(got, get, shift):
    turned = _dot(get[0], got[0]) + _dot(get[1], got[1])
    return _rotate(turned, (L - shift) & 127)


def send_back(back, put, shift):
    turned = _rotate(back, shift).astype(BF16)
    return [_dot(put[j], turned).astype(BF16) for j in range(2)]


CHUNK = 16
NORMAL_STEP = 8
GROUP = 8


def rhs_kernel(
    tile_hbm, offset_hbm, tod_hbm, weight_hbm, beam_hbm, message_ref,
    tile_ref, offset_ref, tod_ref, weight_ref, beam_ref, weighted, back, scratch, small_sems, sems,
):
    small = [
        pltpu.make_async_copy(src, dst, small_sems.at[k])
        for k, (src, dst) in enumerate(
            (
                (tod_hbm, tod_ref),
                (weight_hbm, weight_ref),
                (tile_hbm, tile_ref),
                (offset_hbm, offset_ref),
            )
        )
    ]
    chunks = L // CHUNK

    def beam_copy(c):
        at = pl.ds(pl.multiple_of(c * CHUNK, CHUNK), CHUNK)
        return pltpu.make_async_copy(beam_hbm.at[at], beam_ref.at[at], sems.at[c])

    for copy in small:
        copy.start()
    for c in range(chunks):
        beam_copy(c).start()
    for copy in small:
        copy.wait()
    weighted[...] = (weight_ref[...] * tod_ref[...].astype(F32)).astype(BF16)
    row = _iota((CHUNK, FOOT), 0)

    @pl.loop(0, chunks)
    def _(c):
        beam_copy(c).wait()
        first = pl.multiple_of(c * CHUNK, CHUNK)
        left = weighted[pl.ds(first, CHUNK), :]
        out = jnp.zeros((CHUNK, FOOT), F32)
        for k in range(0, CHUNK, 2):
            two = jnp.concatenate([beam_ref[first + k], beam_ref[first + k + 1]], axis=1)
            found = _dot(left, two)
            out = jnp.where(row == k, found[:, :FOOT], jnp.where(row == k + 1, found[:, FOOT:], out))
        back[pl.ds(first, CHUNK), :] = out

    parts = first_message(
        _as_row(tile_ref[...], scratch), _as_row(offset_ref[...], scratch), back[...]
    )
    for k in range(3):
        message_ref[k] = parts[k]


def normal_kernel(tile_ref, offset_ref, weight_ref, beam_ref, normal_ref, get_ref, put_ref, shift_ref, scratch):
    for k in range(NORMAL_STEP):
        for det in range(2):
            beam = beam_ref[det, k]
            turned = beam.astype(F32).T * weight_ref[det, k : k + 1, :]
            normal_ref[k // 2, det * FOOT : (det + 1) * FOOT, k % 2 * FOOT : (k % 2 + 1) * FOOT] = _dot(
                turned.astype(BF16), beam
            ).astype(BF16)

    @pl.when(pl.program_id(0) == 0)
    def _():
        tile_row = _as_row(tile_ref[...], scratch)
        offset_row = _as_row(offset_ref[...], scratch)
        get, put, shift = block_tables(tile_row, offset_row)
        for j in range(2):
            get_ref[j] = get[j]
            put_ref[j] = put[j]
        shift_ref[...] = shift


def fetch_normal(normal_hbm, normal, sems):
    quads = GROUP // 2

    def copy(g):
        at = pl.ds(g * quads, quads)
        return pltpu.make_async_copy(normal_hbm.at[at], normal.at[at], sems.at[g])

    return [copy(g) for g in range(L // 2 // GROUP)]


def apply_normal(copies, normal, foot, back):
    row = _iota((2 * GROUP, FOOT), 0) & (GROUP - 1)
    none = jnp.zeros((GROUP, FOOT), F32)
    half = L // 2
    for g in range(half // GROUP):
        first = foot[g * GROUP : (g + 1) * GROUP]
        second = foot[half + g * GROUP : half + (g + 1) * GROUP]
        left = jnp.concatenate(
            [jnp.concatenate([first, none], axis=0), jnp.concatenate([none, second], axis=0)], axis=1
        ).astype(BF16)
        out = jnp.zeros((2 * GROUP, FOOT), F32)
        copies[g].wait()
        for k in range(0, GROUP, 2):
            found = _dot(left, normal[(g * GROUP + k) // 2])
            out = jnp.where(row == k, found[:, :FOOT], jnp.where(row == k + 1, found[:, FOOT:], out))
        back[g * GROUP : (g + 1) * GROUP] = out[:GROUP]
        back[half + g * GROUP : half + (g + 1) * GROUP] = out[GROUP:]
    return back[...]


def start_kernel(got_ref, field_ref, message_ref, pick_ref, place_ref, shift_ref):
    pick, place, shifts = owner_tables(got_ref[2])
    field = add_up((got_ref[0], got_ref[1]), place, shifts)
    replies = reply(field, pick, shifts)
    field_ref[...] = field
    message_ref[0] = replies[0]
    message_ref[1] = replies[1]
    message_ref[2] = jnp.broadcast_to(edge_row(field), (L, L)).astype(BF16)
    for k in range(4):
        pick_ref[k] = pick[k]
        place_ref[k] = place[k]
    for j in range(2):
        shift_ref[j] = shifts[j]


def first_apply_kernel(
    got_ref, get_ref, put_ref, shift_ref, normal_hbm, message_ref, foot_ref, back, normal, sems
):
    copies = fetch_normal(normal_hbm, normal, sems)
    for copy in copies:
        copy.start()
    shift = shift_ref[...]
    foot = take_reply((got_ref[0], got_ref[1]), (get_ref[0], get_ref[1]), shift)
    foot_ref[...] = foot
    parts = send_back(
        apply_normal(copies, normal, foot, back), (put_ref[0], put_ref[1]), shift
    )
    message_ref[0] = parts[0]
    message_ref[1] = parts[1]


def middle_kernel(got_ref, before_ref, field_ref, neighbour_ref, pick_ref, place_ref, shift_ref, image_ref, prior_ref, message_ref):
    field = field_ref[...]
    pick = [pick_ref[k] for k in range(4)]
    place = [place_ref[k] for k in range(4)]
    shifts = [shift_ref[j] for j in range(2)]
    before, after = outer_edges(before_ref[2], neighbour_ref[...])
    smooth = prior(field, before, after)
    image = add_up((got_ref[0], got_ref[1]), place, shifts) + smooth
    replies = reply(image, pick, shifts)
    prior_ref[...] = smooth
    image_ref[...] = image
    message_ref[0] = replies[0]
    message_ref[1] = replies[1]
    extra = (
        edge_row(image)
        + _pieces(_total(field * field), SCALARS)
        + _pieces(_total(field * image), SCALARS + 3)
    )
    message_ref[2] = jnp.broadcast_to(extra, (L, L)).astype(BF16)


def second_apply_kernel(
    got_ref, get_ref, put_ref, shift_ref, normal_hbm, foot_ref, field_ref, image_ref, smooth_ref, neighbour_ref,
    message_ref, residual_ref, prior_ref, sums_ref, back, normal, sems,
):
    copies = fetch_normal(normal_hbm, normal, sems)
    for copy in copies:
        copy.start()
    shift = shift_ref[...]
    sums = jnp.sum(got_ref[2].astype(F32), axis=0, keepdims=True)
    sums_ref[...] = sums
    step = _whole(sums, SCALARS) / _whole(sums, SCALARS + 3)
    taken = take_reply((got_ref[0], got_ref[1]), (get_ref[0], get_ref[1]), shift)
    foot = (foot_ref[...] - step * taken).astype(BF16).astype(F32)
    image = image_ref[...]
    before, after = outer_edges(got_ref[2], neighbour_ref[...])
    residual = field_ref[...] - step * image
    smooth = smooth_ref[...] - step * prior(image, before, after)
    residual_ref[...] = residual
    prior_ref[...] = smooth
    turned = apply_normal(copies, normal, foot, back)
    parts = send_back(turned, (put_ref[0], put_ref[1]), shift)
    message_ref[0] = parts[0]
    message_ref[1] = parts[1]
    square = _total(residual * residual)
    product = _total(foot * turned + residual * smooth)
    extra = _pieces(square, SCALARS) + _pieces(product, SCALARS + 3)
    message_ref[2] = jnp.broadcast_to(extra, (L, L)).astype(BF16)


def last_kernel(got_ref, place_ref, shift_ref, field_ref, image_ref, residual_ref, smooth_ref, sums_ref, solution_ref, rest_ref):
    place = [place_ref[k] for k in range(4)]
    shifts = [shift_ref[j] for j in range(2)]
    residual = residual_ref[...]
    field = field_ref[...]
    image = add_up((got_ref[0], got_ref[1]), place, shifts) + smooth_ref[...]
    sums = sums_ref[...]
    more = jnp.sum(got_ref[2].astype(F32), axis=0, keepdims=True)
    norm_first = _whole(sums, SCALARS)
    step_first = norm_first / _whole(sums, SCALARS + 3)
    norm = _whole(more, SCALARS)
    ratio = norm / norm_first
    step = norm / (_whole(more, SCALARS + 3) - ratio * norm / step_first)
    solution = step_first * field + step * (residual + ratio * field)
    rest = residual - step * (image + ratio * image_ref[...])
    for q in range(8):
        solution_ref[:, q * L : (q + 1) * L] = solution[q * TILE : (q + 1) * TILE]
        rest_ref[:, q * L : (q + 1) * L] = rest[q * TILE : (q + 1) * TILE]


def _shape(shape, dtype):
    return jax.ShapeDtypeStruct(shape, dtype)


def _full(shape):
    return pl.BlockSpec(shape, lambda g: (0,) * len(shape))


MAP = (L, L)
WIDE = _shape(MAP, F32)


def call(kernel, grid, in_specs, outs, out_specs, scratch, args, flops, size, vmem):
    return pl.pallas_call(
        kernel,
        grid=grid,
        in_specs=in_specs,
        out_specs=out_specs,
        out_shape=outs,
        scratch_shapes=scratch,
        compiler_params=pltpu.CompilerParams(vmem_limit_bytes=vmem * 2**20),
        cost_estimate=pl.CostEstimate(flops=flops, bytes_accessed=size, transcendentals=0),
    )(*args)


def whole_call(kernel, outs, args, scratch=(), flops=2**25, size=2**19, hbm=()):
    vmem = pl.BlockSpec(memory_space=pltpu.VMEM)
    specs = [
        pl.BlockSpec(memory_space=pltpu.HBM) if k in hbm else vmem for k in range(len(args))
    ]
    return call(kernel, (), specs, outs, [vmem] * len(outs), scratch, args, flops, size, 8)


NORMAL_SCRATCH = [
    pltpu.VMEM(MAP, F32),
    pltpu.VMEM((L // 4, 2 * FOOT, 2 * FOOT), BF16),
    pltpu.SemaphoreType.DMA((L // 2 // GROUP,)),
]


def in_hbm(x):
    return pltpu.with_memory_space_constraint(x, pltpu.HBM)


def exchange(x):
    return lax.all_to_all(x, DET_TM, split_axis=1, concat_axis=1, tiled=True)


def per_device(tod, pointing, weights, tile_ids, offsets, neighbours):
    half = L // 2
    neighbours = neighbours.T

    (message,) = call(
        rhs_kernel,
        (),
        [pl.BlockSpec(memory_space=pltpu.HBM)] * 5,
        [_shape((3, L, L), BF16)],
        [pl.BlockSpec(memory_space=pltpu.VMEM)],
        [
            pltpu.VMEM(tile_ids.shape, jnp.int32),
            pltpu.VMEM(offsets.shape, jnp.int32),
            pltpu.VMEM((L, SAMP), BF16),
            pltpu.VMEM((L, SAMP), F32),
            pltpu.VMEM((L, SAMP, FOOT), BF16),
            pltpu.VMEM((L, SAMP), BF16),
            pltpu.VMEM((L, FOOT), F32),
            pltpu.VMEM((8, L), F32),
            pltpu.SemaphoreType.DMA((4,)),
            pltpu.SemaphoreType.DMA((L // CHUNK,)),
        ],
        (
            in_hbm(tile_ids),
            in_hbm(offsets),
            in_hbm(tod.reshape(L, SAMP)),
            in_hbm(weights.reshape(L, SAMP)),
            in_hbm(pointing.reshape(L, SAMP, FOOT)),
        ),
        2**24,
        2**23,
        16,
    )
    got = exchange(message)

    normal, get, put, shift = call(
        normal_kernel,
        (half // NORMAL_STEP,),
        [_full(tile_ids.shape)] * 2
        + [
            pl.BlockSpec((2, NORMAL_STEP, SAMP), lambda g: (0, g, 0)),
            pl.BlockSpec((2, NORMAL_STEP, SAMP, FOOT), lambda g: (0, g, 0, 0)),
        ],
        [
            pltpu.HBM((half // 2, 2 * FOOT, 2 * FOOT), BF16),
            _shape((2, L, L), BF16),
            _shape((2, L, L), BF16),
            _shape((L, L), jnp.int32),
        ],
        [
            pl.BlockSpec((NORMAL_STEP // 2, 2 * FOOT, 2 * FOOT), lambda g: (g, 0, 0)),
            _full((2, L, L)),
            _full((2, L, L)),
            _full((L, L)),
        ],
        [pltpu.VMEM((8, L), F32)],
        (tile_ids, offsets, weights, in_hbm(pointing)),
        2**30,
        12 * 2**20,
        16,
    )
    normal = in_hbm(normal)
    got, get, put, shift = lax.optimization_barrier((got, get, put, shift))

    field, message, pick, place, shifts = whole_call(
        start_kernel,
        [WIDE, _shape((3, L, L), BF16), _shape((4, L, L), BF16), _shape((4, L, L), BF16), _shape((2, L, L), jnp.int32)],
        (got,),
    )
    got_first = exchange(message)

    message, foot = whole_call(
        first_apply_kernel,
        [_shape((2, L, L), BF16), WIDE],
        (got_first, get, put, shift, normal),
        NORMAL_SCRATCH,
        2**28,
        2**22,
        (4,),
    )
    got = exchange(message)

    image, smooth, message = whole_call(
        middle_kernel,
        [WIDE, WIDE, _shape((3, L, L), BF16)],
        (got, got_first, field, neighbours, pick, place, shifts),
    )
    got = exchange(message)

    message, residual, smooth, sums = whole_call(
        second_apply_kernel,
        [_shape((3, L, L), BF16), WIDE, WIDE, _shape((1, L), F32)],
        (got, get, put, shift, normal, foot, field, image, smooth, neighbours),
        NORMAL_SCRATCH,
        2**28,
        2**22,
        (4,),
    )
    got = exchange(message)

    return tuple(
        whole_call(
            last_kernel,
            [_shape((TILE, 8 * L), F32)] * 2,
            (got, place, shifts, field, image, residual, smooth, sums),
        )
    )


def solution(mesh):
    split = Mesh(mesh.devices.reshape(mesh.shape["det"], 4, 4, 2), DET_TM)
    in_specs = (
        P("det", TM, None),
        P("det", TM, None, None),
        P("det", TM, None),
        P("det", TM),
        P("det", TM),
        P(DET_TM, None),
    )
    out_specs = (P(DET_TM, None), P(DET_TM, None))
    return jax.shard_map(
        per_device, mesh=split, in_specs=in_specs, out_specs=out_specs, check_vma=False
    )
```

```python
import jax
import jax.numpy as jnp
from jax import lax
from jax.experimental import pallas as pl
from jax.experimental.pallas import tpu as pltpu
from jax.sharding import Mesh
from jax.sharding import PartitionSpec as P


DET_TM = ("det", "tm_0", "tm_1", "tm_2")
TM = ("tm_0", "tm_1", "tm_2")
SAMP = 256
FOOT = 128
L = 128
TILE = 16
ROW_STEP = 16
SCALARS = 64

smooth_weight = 2.0
ridge_weight = 0.5

F32 = jnp.float32
BF16 = jnp.bfloat16


def _roll(x, shift, axis):
    return pltpu.roll(x, shift, axis)


def _iota(shape, dim):
    return lax.broadcasted_iota(jnp.int32, shape, dim)


def _dot(a, b):
    return jnp.dot(a, b, preferred_element_type=F32)


def _dot_nt(a, b):
    return lax.dot_general(a, b, (((1,), (1,)), ((), ())), preferred_element_type=F32)


def _onehot(mask):
    return jnp.where(mask, 1.0, 0.0).astype(BF16)


def _to_col(row):
    eye = _iota((L, L), 0) == _iota((L, L), 1)
    return jnp.sum(jnp.where(eye, row, 0.0), axis=1, keepdims=True)


def _to_row(col):
    eye = _iota((L, L), 0) == _iota((L, L), 1)
    return jnp.sum(jnp.where(eye, col, 0.0), axis=0, keepdims=True)


def _rotate(x, amount):
    for bit in range(7):
        x = jnp.where((amount & (1 << bit)) != 0, _roll(x, 1 << bit, 1), x)
    return x


def _as_row(ids, scratch):
    scratch[...] = jnp.zeros(scratch.shape, F32)
    scratch[0:2, 0:64] = ids.astype(F32)
    x = scratch[...]
    return x[0:1] + _roll(x, 64, 1)[1:2]


def _pieces(value, first):
    hi = value.astype(BF16).astype(F32)
    mid = (value - hi).astype(BF16).astype(F32)
    lo = value - hi - mid
    lane = _iota((1, L), 1)
    return jnp.where(
        lane == first, hi, jnp.where(lane == first + 1, mid, jnp.where(lane == first + 2, lo, 0.0))
    )


def _whole(row, first):
    lane = _iota((1, L), 1)
    return jnp.sum(
        jnp.where((lane >= first) & (lane < first + 3), row, 0.0), axis=1, keepdims=True
    )


def _total(x):
    return jnp.sum(jnp.sum(x, axis=0, keepdims=True), axis=1, keepdims=True)


def _blocks_of(owner_row, j):
    block = _iota((L, L), 1)
    return _onehot((_iota((L, L), 0) == owner_row) & ((block & 1) == j))


def places(tile_row, offset_row, put):
    tile = tile_row.astype(jnp.int32)
    offset = offset_row.astype(jnp.int32)
    start_row = (offset >> 7) * ROW_STEP + (tile & 15)
    line = _iota((L, L), 0)
    place = 2 * (_iota((L, L), 1) & 1)
    facts = jnp.where(
        line == place,
        start_row.astype(F32),
        jnp.where(line == place + 1, (offset & 127).astype(F32), 0.0),
    ).astype(BF16)
    return _dot_nt(put[0] + put[1], facts).astype(BF16)


def block_tables(tile_row, offset_row):
    owner = tile_row.astype(jnp.int32) >> 4
    shift = offset_row.astype(jnp.int32) & 127
    owner_col = _to_col(owner.astype(F32)).astype(jnp.int32)
    shift_col = _to_col(shift.astype(F32)).astype(jnp.int32)
    block = _iota((L, L), 0)
    device = _iota((L, L), 1)
    get = [_onehot((device == owner_col) & ((block & 1) == j)) for j in range(2)]
    put = [_blocks_of(owner, j) for j in range(2)]
    return get, put, jnp.broadcast_to(shift_col, (L, L))


def owner_tables(facts):
    facts = facts.astype(F32)
    pick, place, shifts = [], [], []
    for j in range(2):
        start_col = facts[:, 2 * j : 2 * j + 1]
        start_row = _to_row(start_col)
        for step in (0, ROW_STEP):
            pick.append(_onehot(_iota((L, L), 1).astype(F32) == start_col + step))
            place.append(_onehot(_iota((L, L), 0).astype(F32) == start_row + step))
        shifts.append(jnp.broadcast_to(facts[:, 2 * j + 1 : 2 * j + 2], (L, L)).astype(jnp.int32))
    return pick, place, shifts


def add_up(got, place, shifts):
    lane = _iota((L, L), 1)
    total = None
    for j in range(2):
        x = got[j].astype(F32)
        upper = jnp.where(lane >= shifts[j], x, 0.0).astype(BF16)
        lower = jnp.where(lane < shifts[j], x, 0.0).astype(BF16)
        part = _dot(place[2 * j], upper) + _dot(place[2 * j + 1], lower)
        total = part if total is None else total + part
    return total


def reply(field, pick, shifts):
    lane = _iota((L, L), 1)
    field = field.astype(BF16)
    return [
        jnp.where(
            lane >= shifts[j], _dot(pick[2 * j], field), _dot(pick[2 * j + 1], field)
        ).astype(BF16)
        for j in range(2)
    ]


def edge_row(field):
    lane = _iota((TILE, L), 1)
    tile = _iota((TILE, L), 0)
    first = field[0:TILE, 0:1]
    last = field[L - TILE : L, L - 1 : L]
    out = jnp.zeros((TILE, L), F32)
    for k, value in enumerate((first, last)):
        hi = value.astype(BF16).astype(F32)
        out = out + jnp.where(lane == tile + 32 * k, hi, 0.0)
        out = out + jnp.where(lane == tile + 32 * k + 16, value - hi, 0.0)
    return jnp.sum(out, axis=0, keepdims=True)


def outer_edges(edges, neighbours):
    lane = _iota((TILE, L), 1)
    found = []
    for side, base in ((0, 32), (1, 0)):
        line = neighbours[side : side + 1].astype(F32)
        own = _iota((TILE, TILE), 0) == _iota((TILE, TILE), 1)
        tile = jnp.sum(jnp.where(own, line, 0.0), axis=1, keepdims=True).astype(jnp.int32)
        rows = _dot(_onehot(lane == (tile >> 4)), edges)
        at = base + (tile & 15)
        found.append(
            jnp.sum(jnp.where((lane == at) | (lane == at + 16), rows, 0.0), axis=1, keepdims=True)
        )
    return found


def prior(field, before, after):
    lane = _iota((L, L), 1)
    row = _iota((L, L), 0)
    to_right = _roll(field, 1, 1)
    to_left = _roll(field, L - 1, 1)
    left_in = _roll(to_right, ROW_STEP, 0)
    right_in = _roll(to_left, L - ROW_STEP, 0)
    pad = jnp.zeros((L - TILE, 1), F32)
    left_in = jnp.where(row < TILE, jnp.concatenate([before, pad], axis=0), left_in)
    right_in = jnp.where(row >= L - TILE, jnp.concatenate([pad, after], axis=0), right_in)
    lefts = jnp.where(lane == 0, left_in, to_right)
    rights = jnp.where(lane == L - 1, right_in, to_left)
    return smooth_weight * (2.0 * field - lefts - rights) + ridge_weight * field


def take_reply(got, get, shift):
    turned = _dot(get[0], got[0]) + _dot(get[1], got[1])
    return _rotate(turned, (L - shift) & 127)


def send_back(back, put, shift):
    turned = _rotate(back, shift).astype(BF16)
    return [_dot(put[j], turned).astype(BF16) for j in range(2)]


CHUNK = 16
STEPS = (32, 32, 32, 32)
DEPTH = 2


def rhs_kernel(
    tile_hbm, offset_hbm, tod_hbm, weight_hbm, beam_hbm,
    message_ref, normal_ref, get_ref, put_ref, shift_ref,
    tile_ref, offset_ref, tod_ref, weight_ref, beam_ref, weighted, back, scratch, small_sems, sems,
):
    small = [
        pltpu.make_async_copy(src, dst, small_sems.at[k])
        for k, (src, dst) in enumerate(
            (
                (tile_hbm, tile_ref),
                (offset_hbm, offset_ref),
                (tod_hbm, tod_ref),
                (weight_hbm, weight_ref),
            )
        )
    ]
    starts = [sum(STEPS[:k]) for k in range(len(STEPS))]
    beams = [
        pltpu.make_async_copy(
            beam_hbm.at[pl.ds(first, size)], beam_ref.at[pl.ds(first, size)], sems.at[k]
        )
        for k, (first, size) in enumerate(zip(starts, STEPS))
    ]

    for copy in small:
        copy.start()
    for copy in beams[:DEPTH]:
        copy.start()
    small[0].wait()
    small[1].wait()
    tile_row = _as_row(tile_ref[...], scratch)
    offset_row = _as_row(offset_ref[...], scratch)
    get, put, shift = block_tables(tile_row, offset_row)
    for j in range(2):
        get_ref[j] = get[j]
        put_ref[j] = put[j]
    shift_ref[...] = shift
    message_ref[2] = places(tile_row, offset_row, put)
    small[2].wait()
    small[3].wait()
    weighted[...] = (weight_ref[...] * tod_ref[...].astype(F32)).astype(BF16)
    row = _iota((CHUNK, FOOT), 0)

    for step, (start, size) in enumerate(zip(starts, STEPS)):
        beams[step].wait()
        if step + DEPTH < len(STEPS):
            beams[step + DEPTH].start()
        for first in range(start, start + size, CHUNK):
            rows = weighted[first : first + CHUNK]
            weight = weight_ref[first : first + CHUNK]
            out = jnp.zeros((CHUNK, FOOT), F32)
            for k in range(CHUNK):
                beam = beam_ref[first + k]
                turned = (beam.T.astype(F32) * weight[k : k + 1]).astype(BF16)
                found = _dot(jnp.concatenate([turned, rows], axis=0), beam)
                down, across = k % 2 * FOOT, k // 2 % 2 * FOOT
                normal_ref[(first + k) // 4, down : down + FOOT, across : across + FOOT] = found[
                    :FOOT
                ].astype(BF16)
                out = jnp.where(row == k, found[FOOT:], out)
            back[first : first + CHUNK] = out

    parts = send_back(back[...], put, shift)
    message_ref[0] = parts[0]
    message_ref[1] = parts[1]


def apply_normal(normal_ref, foot, back):
    row = _iota((CHUNK, FOOT), 0)
    for c in range(L // CHUNK):
        own = foot[c * CHUNK : (c + 1) * CHUNK]
        left = jnp.concatenate(
            [jnp.where((row & 1) == 0, own, 0.0), jnp.where((row & 1) == 1, own, 0.0)], axis=1
        ).astype(BF16)
        out = jnp.zeros((CHUNK, FOOT), F32)
        for q in range(CHUNK // 4):
            found = _dot(left, normal_ref[c * (CHUNK // 4) + q])
            out = jnp.where(
                (row >> 1) == 2 * q, found[:, :FOOT], jnp.where((row >> 1) == 2 * q + 1, found[:, FOOT:], out)
            )
        back[c * CHUNK : (c + 1) * CHUNK] = out
    return back[...]


def start_kernel(got_ref, field_ref, message_ref, pick_ref, place_ref, shift_ref):
    pick, place, shifts = owner_tables(got_ref[2])
    field = add_up((got_ref[0], got_ref[1]), place, shifts)
    replies = reply(field, pick, shifts)
    field_ref[...] = field
    message_ref[0] = replies[0]
    message_ref[1] = replies[1]
    message_ref[2] = jnp.broadcast_to(edge_row(field), (L, L)).astype(BF16)
    for k in range(4):
        pick_ref[k] = pick[k]
        place_ref[k] = place[k]
    for j in range(2):
        shift_ref[j] = shifts[j]


def first_apply_kernel(
    got_ref, get_ref, put_ref, shift_ref, normal_ref, message_ref, foot_ref, back
):
    shift = shift_ref[...]
    foot = take_reply((got_ref[0], got_ref[1]), (get_ref[0], get_ref[1]), shift)
    foot_ref[...] = foot
    parts = send_back(
        apply_normal(normal_ref, foot, back), (put_ref[0], put_ref[1]), shift
    )
    message_ref[0] = parts[0]
    message_ref[1] = parts[1]


def middle_kernel(got_ref, before_ref, field_ref, neighbour_ref, pick_ref, place_ref, shift_ref, image_ref, prior_ref, message_ref):
    field = field_ref[...]
    pick = [pick_ref[k] for k in range(4)]
    place = [place_ref[k] for k in range(4)]
    shifts = [shift_ref[j] for j in range(2)]
    before, after = outer_edges(before_ref[2], neighbour_ref[...])
    smooth = prior(field, before, after)
    image = add_up((got_ref[0], got_ref[1]), place, shifts) + smooth
    replies = reply(image, pick, shifts)
    prior_ref[...] = smooth
    image_ref[...] = image
    message_ref[0] = replies[0]
    message_ref[1] = replies[1]
    extra = (
        edge_row(image)
        + _pieces(_total(field * field), SCALARS)
        + _pieces(_total(field * image), SCALARS + 3)
    )
    message_ref[2] = jnp.broadcast_to(extra, (L, L)).astype(BF16)


def second_apply_kernel(
    got_ref, get_ref, put_ref, shift_ref, normal_ref, foot_ref, field_ref, image_ref, smooth_ref, neighbour_ref,
    message_ref, residual_ref, prior_ref, sums_ref, back,
):
    shift = shift_ref[...]
    sums = jnp.sum(got_ref[2].astype(F32), axis=0, keepdims=True)
    sums_ref[...] = sums
    step = _whole(sums, SCALARS) / _whole(sums, SCALARS + 3)
    taken = take_reply((got_ref[0], got_ref[1]), (get_ref[0], get_ref[1]), shift)
    foot = (foot_ref[...] - step * taken).astype(BF16).astype(F32)
    image = image_ref[...]
    before, after = outer_edges(got_ref[2], neighbour_ref[...])
    residual = field_ref[...] - step * image
    smooth = smooth_ref[...] - step * prior(image, before, after)
    residual_ref[...] = residual
    prior_ref[...] = smooth
    turned = apply_normal(normal_ref, foot, back)
    parts = send_back(turned, (put_ref[0], put_ref[1]), shift)
    message_ref[0] = parts[0]
    message_ref[1] = parts[1]
    square = _total(residual * residual)
    product = _total(foot * turned + residual * smooth)
    extra = _pieces(square, SCALARS) + _pieces(product, SCALARS + 3)
    message_ref[2] = jnp.broadcast_to(extra, (L, L)).astype(BF16)


def last_kernel(got_ref, place_ref, shift_ref, field_ref, image_ref, residual_ref, smooth_ref, sums_ref, solution_ref, rest_ref):
    place = [place_ref[k] for k in range(4)]
    shifts = [shift_ref[j] for j in range(2)]
    residual = residual_ref[...]
    field = field_ref[...]
    image = add_up((got_ref[0], got_ref[1]), place, shifts) + smooth_ref[...]
    sums = sums_ref[...]
    more = jnp.sum(got_ref[2].astype(F32), axis=0, keepdims=True)
    norm_first = _whole(sums, SCALARS)
    step_first = norm_first / _whole(sums, SCALARS + 3)
    norm = _whole(more, SCALARS)
    ratio = norm / norm_first
    step = norm / (_whole(more, SCALARS + 3) - ratio * norm / step_first)
    solution = step_first * field + step * (residual + ratio * field)
    rest = residual - step * (image + ratio * image_ref[...])
    for q in range(8):
        solution_ref[:, q * L : (q + 1) * L] = solution[q * TILE : (q + 1) * TILE]
        rest_ref[:, q * L : (q + 1) * L] = rest[q * TILE : (q + 1) * TILE]


def _shape(shape, dtype):
    return jax.ShapeDtypeStruct(shape, dtype)


def _full(shape):
    return pl.BlockSpec(shape, lambda g: (0,) * len(shape))


MAP = (L, L)
WIDE = _shape(MAP, F32)


def call(kernel, grid, in_specs, outs, out_specs, scratch, args, flops, size, vmem):
    return pl.pallas_call(
        kernel,
        grid=grid,
        in_specs=in_specs,
        out_specs=out_specs,
        out_shape=outs,
        scratch_shapes=scratch,
        compiler_params=pltpu.CompilerParams(vmem_limit_bytes=vmem * 2**20),
        cost_estimate=pl.CostEstimate(flops=flops, bytes_accessed=size, transcendentals=0),
    )(*args)


def whole_call(kernel, outs, args, scratch=(), flops=2**25, size=2**19):
    vmem = pl.BlockSpec(memory_space=pltpu.VMEM)
    return call(
        kernel, (), [vmem] * len(args), outs, [vmem] * len(outs), scratch, args, flops, size, 8
    )


def in_hbm(x):
    return pltpu.with_memory_space_constraint(x, pltpu.HBM)


def exchange(x):
    return lax.all_to_all(x, DET_TM, split_axis=1, concat_axis=1, tiled=True)


def per_device(tod, pointing, weights, tile_ids, offsets, neighbours):
    neighbours = neighbours.T

    message, normal, get, put, shift = call(
        rhs_kernel,
        (),
        [pl.BlockSpec(memory_space=pltpu.HBM)] * 5,
        [
            _shape((3, L, L), BF16),
            pltpu.VMEM((L // 4, 2 * FOOT, 2 * FOOT), BF16),
            _shape((2, L, L), BF16),
            _shape((2, L, L), BF16),
            _shape((L, L), jnp.int32),
        ],
        [pl.BlockSpec(memory_space=pltpu.VMEM)] * 5,
        [
            pltpu.VMEM(tile_ids.shape, jnp.int32),
            pltpu.VMEM(offsets.shape, jnp.int32),
            pltpu.VMEM((L, SAMP), BF16),
            pltpu.VMEM((L, SAMP), F32),
            pltpu.VMEM((L, SAMP, FOOT), BF16),
            pltpu.VMEM((L, SAMP), BF16),
            pltpu.VMEM((L, FOOT), F32),
            pltpu.VMEM((8, L), F32),
            pltpu.SemaphoreType.DMA((4,)),
            pltpu.SemaphoreType.DMA((len(STEPS),)),
        ],
        (
            in_hbm(tile_ids),
            in_hbm(offsets),
            in_hbm(tod.reshape(L, SAMP)),
            in_hbm(weights.reshape(L, SAMP)),
            in_hbm(pointing.reshape(L, SAMP, FOOT)),
        ),
        2**30,
        2**23,
        16,
    )
    got = exchange(message)

    field, message, pick, place, shifts = whole_call(
        start_kernel,
        [WIDE, _shape((3, L, L), BF16), _shape((4, L, L), BF16), _shape((4, L, L), BF16), _shape((2, L, L), jnp.int32)],
        (got,),
    )
    got_first = exchange(message)

    message, foot = whole_call(
        first_apply_kernel,
        [_shape((2, L, L), BF16), WIDE],
        (got_first, get, put, shift, normal),
        [pltpu.VMEM(MAP, F32)],
        2**28,
        2**22,
    )
    got = exchange(message)

    image, smooth, message = whole_call(
        middle_kernel,
        [WIDE, WIDE, _shape((3, L, L), BF16)],
        (got, got_first, field, neighbours, pick, place, shifts),
    )
    got = exchange(message)

    message, residual, smooth, sums = whole_call(
        second_apply_kernel,
        [_shape((3, L, L), BF16), WIDE, WIDE, _shape((1, L), F32)],
        (got, get, put, shift, normal, foot, field, image, smooth, neighbours),
        [pltpu.VMEM(MAP, F32)],
        2**28,
        2**22,
    )
    got = exchange(message)

    return tuple(
        whole_call(
            last_kernel,
            [_shape((TILE, 8 * L), F32)] * 2,
            (got, place, shifts, field, image, residual, smooth, sums),
        )
    )


def solution(mesh):
    split = Mesh(mesh.devices.reshape(mesh.shape["det"], 4, 4, 2), DET_TM)
    in_specs = (
        P("det", TM, None),
        P("det", TM, None, None),
        P("det", TM, None),
        P("det", TM),
        P("det", TM),
        P(DET_TM, None),
    )
    out_specs = (P(DET_TM, None), P(DET_TM, None))
    return jax.shard_map(
        per_device, mesh=split, in_specs=in_specs, out_specs=out_specs, check_vma=False
    )
```

```python
import jax
import jax.numpy as jnp
from jax import lax
from jax.experimental import pallas as pl
from jax.experimental.pallas import tpu as pltpu
from jax.sharding import Mesh
from jax.sharding import PartitionSpec as P


DET_TM = ("det", "tm_0", "tm_1", "tm_2")
TM = ("tm_0", "tm_1", "tm_2")
SEND = ("tm_2", "tm_1", "tm_0", "det")
SAMP = 256
FOOT = 128
L = 128
TILE = 16
ROW_STEP = 16
SCALARS = 64

smooth_weight = 2.0
ridge_weight = 0.5

F32 = jnp.float32
BF16 = jnp.bfloat16


def _roll(x, shift, axis):
    return pltpu.roll(x, shift, axis)


def _iota(shape, dim):
    return lax.broadcasted_iota(jnp.int32, shape, dim)


def _dot(a, b):
    return jnp.dot(a, b, preferred_element_type=F32)


def _dot_nt(a, b):
    return lax.dot_general(a, b, (((1,), (1,)), ((), ())), preferred_element_type=F32)


def _onehot(mask):
    return jnp.where(mask, 1.0, 0.0).astype(BF16)


def _to_col(row):
    eye = _iota((L, L), 0) == _iota((L, L), 1)
    return jnp.sum(jnp.where(eye, row, 0.0), axis=1, keepdims=True)


def _to_row(col):
    eye = _iota((L, L), 0) == _iota((L, L), 1)
    return jnp.sum(jnp.where(eye, col, 0.0), axis=0, keepdims=True)


def _rotate(x, amount):
    step = 1
    for base in (8, 4, 4):
        digit = (amount >> (step.bit_length() - 1)) & (base - 1)
        turned = x
        for value in range(1, base):
            turned = jnp.where(digit == value, _roll(x, step * value, 1), turned)
        x = turned
        step *= base
    return x


def _as_row(ids, scratch):
    scratch[...] = jnp.zeros(scratch.shape, F32)
    scratch[0:2, 0:64] = ids.astype(F32)
    x = scratch[...]
    return x[0:1] + _roll(x, 64, 1)[1:2]


def _pieces(value, first):
    hi = value.astype(BF16).astype(F32)
    mid = (value - hi).astype(BF16).astype(F32)
    lo = value - hi - mid
    lane = _iota((1, L), 1)
    return jnp.where(
        lane == first, hi, jnp.where(lane == first + 1, mid, jnp.where(lane == first + 2, lo, 0.0))
    )


def _whole(row, first):
    lane = _iota((1, L), 1)
    return jnp.sum(
        jnp.where((lane >= first) & (lane < first + 3), row, 0.0), axis=1, keepdims=True
    )


def _total(x):
    return jnp.sum(jnp.sum(x, axis=0, keepdims=True), axis=1, keepdims=True)


def _owner(tile):
    det, tm_0, tm_1, tm_2 = tile >> 9, (tile >> 7) & 3, (tile >> 5) & 3, (tile >> 4) & 1
    return (tm_2 << 6) | (tm_1 << 4) | (tm_0 << 2) | det


def _blocks_of(owner_row, j):
    block = _iota((L, L), 1)
    return _onehot((_iota((L, L), 0) == owner_row) & ((block & 1) == j))


def places(tile_row, offset_row, put):
    tile = tile_row.astype(jnp.int32)
    offset = offset_row.astype(jnp.int32)
    start_row = (offset >> 7) * ROW_STEP + (tile & 15)
    line = _iota((L, L), 0)
    place = 2 * (_iota((L, L), 1) & 1)
    facts = jnp.where(
        line == place,
        start_row.astype(F32),
        jnp.where(line == place + 1, (offset & 127).astype(F32), 0.0),
    ).astype(BF16)
    return _dot_nt(put[0] + put[1], facts).astype(BF16)


def block_tables(tile_row, offset_row):
    owner = _owner(tile_row.astype(jnp.int32))
    shift = offset_row.astype(jnp.int32) & 127
    owner_col = _to_col(owner.astype(F32)).astype(jnp.int32)
    shift_col = _to_col(shift.astype(F32)).astype(jnp.int32)
    block = _iota((L, L), 0)
    device = _iota((L, L), 1)
    get = [_onehot((device == owner_col) & ((block & 1) == j)) for j in range(2)]
    put = [_blocks_of(owner, j) for j in range(2)]
    return get, put, jnp.broadcast_to(shift_col, (L, L))


def owner_tables(facts):
    facts = facts.astype(F32)
    pick, place, shifts = [], [], []
    for j in range(2):
        start_col = facts[:, 2 * j : 2 * j + 1]
        start_row = _to_row(start_col)
        for step in (0, ROW_STEP):
            pick.append(_onehot(_iota((L, L), 1).astype(F32) == start_col + step))
            place.append(_onehot(_iota((L, L), 0).astype(F32) == start_row + step))
        shifts.append(jnp.broadcast_to(facts[:, 2 * j + 1 : 2 * j + 2], (L, L)).astype(jnp.int32))
    return pick, place, shifts


def add_up(got, place, shifts):
    lane = _iota((L, L), 1)
    total = None
    for j in range(2):
        x = got[j].astype(F32)
        upper = jnp.where(lane >= shifts[j], x, 0.0).astype(BF16)
        lower = jnp.where(lane < shifts[j], x, 0.0).astype(BF16)
        part = _dot(place[2 * j], upper) + _dot(place[2 * j + 1], lower)
        total = part if total is None else total + part
    return total


def reply(field, pick, shifts):
    lane = _iota((L, L), 1)
    field = field.astype(BF16)
    return [
        jnp.where(
            lane >= shifts[j], _dot(pick[2 * j], field), _dot(pick[2 * j + 1], field)
        ).astype(BF16)
        for j in range(2)
    ]


def edge_row(field):
    lane = _iota((TILE, L), 1)
    tile = _iota((TILE, L), 0)
    first = field[0:TILE, 0:1]
    last = field[L - TILE : L, L - 1 : L]
    out = jnp.zeros((TILE, L), F32)
    for k, value in enumerate((first, last)):
        hi = value.astype(BF16).astype(F32)
        out = out + jnp.where(lane == tile + 32 * k, hi, 0.0)
        out = out + jnp.where(lane == tile + 32 * k + 16, value - hi, 0.0)
    return jnp.sum(out, axis=0, keepdims=True)


def outer_edges(edges, neighbours):
    lane = _iota((TILE, L), 1)
    found = []
    for side, base in ((0, 32), (1, 0)):
        line = neighbours[side : side + 1].astype(F32)
        own = _iota((TILE, TILE), 0) == _iota((TILE, TILE), 1)
        tile = jnp.sum(jnp.where(own, line, 0.0), axis=1, keepdims=True).astype(jnp.int32)
        rows = _dot(_onehot(lane == _owner(tile)), edges)
        at = base + (tile & 15)
        found.append(
            jnp.sum(jnp.where((lane == at) | (lane == at + 16), rows, 0.0), axis=1, keepdims=True)
        )
    return found


def prior(field, before, after):
    lane = _iota((L, L), 1)
    row = _iota((L, L), 0)
    to_right = _roll(field, 1, 1)
    to_left = _roll(field, L - 1, 1)
    left_in = _roll(to_right, ROW_STEP, 0)
    right_in = _roll(to_left, L - ROW_STEP, 0)
    pad = jnp.zeros((L - TILE, 1), F32)
    left_in = jnp.where(row < TILE, jnp.concatenate([before, pad], axis=0), left_in)
    right_in = jnp.where(row >= L - TILE, jnp.concatenate([pad, after], axis=0), right_in)
    lefts = jnp.where(lane == 0, left_in, to_right)
    rights = jnp.where(lane == L - 1, right_in, to_left)
    return smooth_weight * (2.0 * field - lefts - rights) + ridge_weight * field


def take_reply(got, get, shift):
    turned = _dot(get[0], got[0]) + _dot(get[1], got[1])
    return _rotate(turned, (L - shift) & 127)


def send_back(back, put, shift):
    turned = _rotate(back, shift).astype(BF16)
    return [_dot(put[j], turned).astype(BF16) for j in range(2)]


CHUNK = 16
STEPS = (32, 32, 32, 32)
DEPTH = 2


def rhs_kernel(
    tile_hbm, offset_hbm, tod_hbm, weight_hbm, beam_hbm,
    message_ref, normal_ref, get_ref, put_ref, shift_ref,
    tile_ref, offset_ref, tod_ref, weight_ref, beam_ref, weighted, back, scratch, small_sems, sems,
):
    small = [
        pltpu.make_async_copy(src, dst, small_sems.at[k])
        for k, (src, dst) in enumerate(
            (
                (tile_hbm, tile_ref),
                (offset_hbm, offset_ref),
                (tod_hbm, tod_ref),
                (weight_hbm, weight_ref),
            )
        )
    ]
    starts = [sum(STEPS[:k]) for k in range(len(STEPS))]
    beams = [
        pltpu.make_async_copy(
            beam_hbm.at[pl.ds(first, size)], beam_ref.at[pl.ds(first, size)], sems.at[k]
        )
        for k, (first, size) in enumerate(zip(starts, STEPS))
    ]

    for copy in small:
        copy.start()
    for copy in beams[:DEPTH]:
        copy.start()
    small[0].wait()
    small[1].wait()
    tile_row = _as_row(tile_ref[...], scratch)
    offset_row = _as_row(offset_ref[...], scratch)
    get, put, shift = block_tables(tile_row, offset_row)
    for j in range(2):
        get_ref[j] = get[j]
        put_ref[j] = put[j]
    shift_ref[...] = shift
    message_ref[2] = places(tile_row, offset_row, put)
    small[2].wait()
    small[3].wait()
    weighted[...] = (weight_ref[...] * tod_ref[...].astype(F32)).astype(BF16)
    row = _iota((CHUNK, FOOT), 0)

    for step, (start, size) in enumerate(zip(starts, STEPS)):
        beams[step].wait()
        if step + DEPTH < len(STEPS):
            beams[step + DEPTH].start()
        for first in range(start, start + size, CHUNK):
            rows = weighted[first : first + CHUNK]
            weight = weight_ref[first : first + CHUNK]
            out = jnp.zeros((CHUNK, FOOT), F32)
            for k in range(CHUNK):
                beam = beam_ref[first + k]
                turned = (beam.T.astype(F32) * weight[k : k + 1]).astype(BF16)
                found = _dot(jnp.concatenate([turned, rows], axis=0), beam)
                down, across = k % 2 * FOOT, k // 2 % 2 * FOOT
                normal_ref[(first + k) // 4, down : down + FOOT, across : across + FOOT] = found[
                    :FOOT
                ].astype(BF16)
                out = jnp.where(row == k, found[FOOT:], out)
            back[first : first + CHUNK] = out

    parts = send_back(back[...], put, shift)
    message_ref[0] = parts[0]
    message_ref[1] = parts[1]


def apply_normal(normal_ref, foot, back):
    row = _iota((CHUNK, FOOT), 0)
    for c in range(L // CHUNK):
        own = foot[c * CHUNK : (c + 1) * CHUNK]
        left = jnp.concatenate(
            [jnp.where((row & 1) == 0, own, 0.0), jnp.where((row & 1) == 1, own, 0.0)], axis=1
        ).astype(BF16)
        out = jnp.zeros((CHUNK, FOOT), F32)
        for q in range(CHUNK // 4):
            found = _dot(left, normal_ref[c * (CHUNK // 4) + q])
            out = jnp.where(
                (row >> 1) == 2 * q, found[:, :FOOT], jnp.where((row >> 1) == 2 * q + 1, found[:, FOOT:], out)
            )
        back[c * CHUNK : (c + 1) * CHUNK] = out
    return back[...]


def start_kernel(got_ref, field_ref, message_ref, pick_ref, place_ref, shift_ref):
    pick, place, shifts = owner_tables(got_ref[2])
    field = add_up((got_ref[0], got_ref[1]), place, shifts)
    replies = reply(field, pick, shifts)
    field_ref[...] = field
    message_ref[0] = replies[0]
    message_ref[1] = replies[1]
    message_ref[2] = jnp.broadcast_to(edge_row(field), (L, L)).astype(BF16)
    for k in range(4):
        pick_ref[k] = pick[k]
        place_ref[k] = place[k]
    for j in range(2):
        shift_ref[j] = shifts[j]


def first_apply_kernel(
    got_ref, get_ref, put_ref, shift_ref, normal_ref, message_ref, foot_ref, back
):
    shift = shift_ref[...]
    foot = take_reply((got_ref[0], got_ref[1]), (get_ref[0], get_ref[1]), shift)
    foot_ref[...] = foot
    parts = send_back(
        apply_normal(normal_ref, foot, back), (put_ref[0], put_ref[1]), shift
    )
    message_ref[0] = parts[0]
    message_ref[1] = parts[1]


def middle_kernel(got_ref, before_ref, field_ref, neighbour_ref, pick_ref, place_ref, shift_ref, image_ref, prior_ref, message_ref):
    field = field_ref[...]
    pick = [pick_ref[k] for k in range(4)]
    place = [place_ref[k] for k in range(4)]
    shifts = [shift_ref[j] for j in range(2)]
    before, after = outer_edges(before_ref[2], neighbour_ref[...])
    smooth = prior(field, before, after)
    image = add_up((got_ref[0], got_ref[1]), place, shifts) + smooth
    replies = reply(image, pick, shifts)
    prior_ref[...] = smooth
    image_ref[...] = image
    message_ref[0] = replies[0]
    message_ref[1] = replies[1]
    extra = (
        edge_row(image)
        + _pieces(_total(field * field), SCALARS)
        + _pieces(_total(field * image), SCALARS + 3)
    )
    message_ref[2] = jnp.broadcast_to(extra, (L, L)).astype(BF16)


def second_apply_kernel(
    got_ref, get_ref, put_ref, shift_ref, normal_ref, foot_ref, field_ref, image_ref, smooth_ref, neighbour_ref,
    message_ref, residual_ref, prior_ref, sums_ref, back,
):
    shift = shift_ref[...]
    sums = jnp.sum(got_ref[2].astype(F32), axis=0, keepdims=True)
    sums_ref[...] = sums
    step = _whole(sums, SCALARS) / _whole(sums, SCALARS + 3)
    taken = take_reply((got_ref[0], got_ref[1]), (get_ref[0], get_ref[1]), shift)
    foot = (foot_ref[...] - step * taken).astype(BF16).astype(F32)
    image = image_ref[...]
    before, after = outer_edges(got_ref[2], neighbour_ref[...])
    residual = field_ref[...] - step * image
    smooth = smooth_ref[...] - step * prior(image, before, after)
    residual_ref[...] = residual
    prior_ref[...] = smooth
    turned = apply_normal(normal_ref, foot, back)
    parts = send_back(turned, (put_ref[0], put_ref[1]), shift)
    message_ref[0] = parts[0]
    message_ref[1] = parts[1]
    square = _total(residual * residual)
    product = _total(foot * turned + residual * smooth)
    extra = _pieces(square, SCALARS) + _pieces(product, SCALARS + 3)
    message_ref[2] = jnp.broadcast_to(extra, (L, L)).astype(BF16)


def last_kernel(got_ref, place_ref, shift_ref, field_ref, image_ref, residual_ref, smooth_ref, sums_ref, solution_ref, rest_ref):
    place = [place_ref[k] for k in range(4)]
    shifts = [shift_ref[j] for j in range(2)]
    residual = residual_ref[...]
    field = field_ref[...]
    image = add_up((got_ref[0], got_ref[1]), place, shifts) + smooth_ref[...]
    sums = sums_ref[...]
    more = jnp.sum(got_ref[2].astype(F32), axis=0, keepdims=True)
    norm_first = _whole(sums, SCALARS)
    step_first = norm_first / _whole(sums, SCALARS + 3)
    norm = _whole(more, SCALARS)
    ratio = norm / norm_first
    step = norm / (_whole(more, SCALARS + 3) - ratio * norm / step_first)
    solution = step_first * field + step * (residual + ratio * field)
    rest = residual - step * (image + ratio * image_ref[...])
    for q in range(8):
        solution_ref[:, q * L : (q + 1) * L] = solution[q * TILE : (q + 1) * TILE]
        rest_ref[:, q * L : (q + 1) * L] = rest[q * TILE : (q + 1) * TILE]


def _shape(shape, dtype):
    return jax.ShapeDtypeStruct(shape, dtype)


def _full(shape):
    return pl.BlockSpec(shape, lambda g: (0,) * len(shape))


MAP = (L, L)
WIDE = _shape(MAP, F32)


def call(kernel, grid, in_specs, outs, out_specs, scratch, args, flops, size, vmem):
    return pl.pallas_call(
        kernel,
        grid=grid,
        in_specs=in_specs,
        out_specs=out_specs,
        out_shape=outs,
        scratch_shapes=scratch,
        compiler_params=pltpu.CompilerParams(vmem_limit_bytes=vmem * 2**20),
        cost_estimate=pl.CostEstimate(flops=flops, bytes_accessed=size, transcendentals=0),
    )(*args)


def whole_call(kernel, outs, args, scratch=(), flops=2**25, size=2**19):
    vmem = pl.BlockSpec(memory_space=pltpu.VMEM)
    return call(
        kernel, (), [vmem] * len(args), outs, [vmem] * len(outs), scratch, args, flops, size, 8
    )


def in_hbm(x):
    return pltpu.with_memory_space_constraint(x, pltpu.HBM)


def exchange(x):
    return lax.all_to_all(x, SEND, split_axis=1, concat_axis=1, tiled=True)


def per_device(tod, pointing, weights, tile_ids, offsets, neighbours):
    neighbours = neighbours.T

    message, normal, get, put, shift = call(
        rhs_kernel,
        (),
        [pl.BlockSpec(memory_space=pltpu.HBM)] * 5,
        [
            _shape((3, L, L), BF16),
            pltpu.VMEM((L // 4, 2 * FOOT, 2 * FOOT), BF16),
            _shape((2, L, L), BF16),
            _shape((2, L, L), BF16),
            _shape((L, L), jnp.int32),
        ],
        [pl.BlockSpec(memory_space=pltpu.VMEM)] * 5,
        [
            pltpu.VMEM(tile_ids.shape, jnp.int32),
            pltpu.VMEM(offsets.shape, jnp.int32),
            pltpu.VMEM((L, SAMP), BF16),
            pltpu.VMEM((L, SAMP), F32),
            pltpu.VMEM((L, SAMP, FOOT), BF16),
            pltpu.VMEM((L, SAMP), BF16),
            pltpu.VMEM((L, FOOT), F32),
            pltpu.VMEM((8, L), F32),
            pltpu.SemaphoreType.DMA((4,)),
            pltpu.SemaphoreType.DMA((len(STEPS),)),
        ],
        (
            in_hbm(tile_ids),
            in_hbm(offsets),
            in_hbm(tod.reshape(L, SAMP)),
            in_hbm(weights.reshape(L, SAMP)),
            in_hbm(pointing.reshape(L, SAMP, FOOT)),
        ),
        2**30,
        2**23,
        16,
    )
    got = exchange(message)

    field, message, pick, place, shifts = whole_call(
        start_kernel,
        [WIDE, _shape((3, L, L), BF16), _shape((4, L, L), BF16), _shape((4, L, L), BF16), _shape((2, L, L), jnp.int32)],
        (got,),
    )
    got_first = exchange(message)

    message, foot = whole_call(
        first_apply_kernel,
        [_shape((2, L, L), BF16), WIDE],
        (got_first, get, put, shift, normal),
        [pltpu.VMEM(MAP, F32)],
        2**28,
        2**22,
    )
    got = exchange(message)

    image, smooth, message = whole_call(
        middle_kernel,
        [WIDE, WIDE, _shape((3, L, L), BF16)],
        (got, got_first, field, neighbours, pick, place, shifts),
    )
    got = exchange(message)

    message, residual, smooth, sums = whole_call(
        second_apply_kernel,
        [_shape((3, L, L), BF16), WIDE, WIDE, _shape((1, L), F32)],
        (got, get, put, shift, normal, foot, field, image, smooth, neighbours),
        [pltpu.VMEM(MAP, F32)],
        2**28,
        2**22,
    )
    got = exchange(message)

    return tuple(
        whole_call(
            last_kernel,
            [_shape((TILE, 8 * L), F32)] * 2,
            (got, place, shifts, field, image, residual, smooth, sums),
        )
    )


def solution(mesh):
    split = Mesh(mesh.devices.reshape(mesh.shape["det"], 4, 4, 2), DET_TM)
    in_specs = (
        P("det", TM, None),
        P("det", TM, None, None),
        P("det", TM, None),
        P("det", TM),
        P("det", TM),
        P(DET_TM, None),
    )
    out_specs = (P(DET_TM, None), P(DET_TM, None))
    return jax.shard_map(
        per_device, mesh=split, in_specs=in_specs, out_specs=out_specs, check_vma=False
    )
```

```python
import jax
import jax.numpy as jnp
from jax import lax
from jax.experimental import pallas as pl
from jax.experimental.pallas import tpu as pltpu
from jax.sharding import Mesh
from jax.sharding import PartitionSpec as P


DET_TM = ("det", "tm_0", "tm_1", "tm_2")
TM = ("tm_0", "tm_1", "tm_2")
SEND = ("tm_2", "tm_1", "tm_0", "det")
SAMP = 256
FOOT = 128
L = 128
TILE = 16
ROW_STEP = 16
SCALARS = 64

smooth_weight = 2.0
ridge_weight = 0.5

F32 = jnp.float32
BF16 = jnp.bfloat16


def _roll(x, shift, axis):
    return pltpu.roll(x, shift, axis)


def _iota(shape, dim):
    return lax.broadcasted_iota(jnp.int32, shape, dim)


def _dot(a, b):
    return jnp.dot(a, b, preferred_element_type=F32)


def _dot_nt(a, b):
    return lax.dot_general(a, b, (((1,), (1,)), ((), ())), preferred_element_type=F32)


def _onehot(mask):
    return jnp.where(mask, 1.0, 0.0).astype(BF16)


def _to_col(row):
    eye = _iota((L, L), 0) == _iota((L, L), 1)
    return jnp.sum(jnp.where(eye, row, 0.0), axis=1, keepdims=True)


def _to_row(col):
    eye = _iota((L, L), 0) == _iota((L, L), 1)
    return jnp.sum(jnp.where(eye, col, 0.0), axis=0, keepdims=True)


def _rotate(x, amount):
    step = 1
    for base in (16, 8):
        digit = (amount >> (step.bit_length() - 1)) & (base - 1)
        turned = x
        for value in range(1, base):
            turned = jnp.where(digit == value, _roll(x, step * value, 1), turned)
        x = turned
        step *= base
    return x


def _as_row(ids, scratch):
    scratch[...] = jnp.zeros(scratch.shape, F32)
    scratch[0:2, 0:64] = ids.astype(F32)
    x = scratch[...]
    return x[0:1] + _roll(x, 64, 1)[1:2]


def _pieces(value, first):
    hi = value.astype(BF16).astype(F32)
    mid = (value - hi).astype(BF16).astype(F32)
    lo = value - hi - mid
    lane = _iota((1, L), 1)
    return jnp.where(
        lane == first, hi, jnp.where(lane == first + 1, mid, jnp.where(lane == first + 2, lo, 0.0))
    )


def _whole(row, first):
    lane = _iota((1, L), 1)
    return jnp.sum(
        jnp.where((lane >= first) & (lane < first + 3), row, 0.0), axis=1, keepdims=True
    )


def _total(x):
    return jnp.sum(jnp.sum(x, axis=0, keepdims=True), axis=1, keepdims=True)


def _owner(tile):
    det, tm_0, tm_1, tm_2 = tile >> 9, (tile >> 7) & 3, (tile >> 5) & 3, (tile >> 4) & 1
    return (tm_2 << 6) | (tm_1 << 4) | (tm_0 << 2) | det


def _blocks_of(owner_row, j):
    block = _iota((L, L), 1)
    return _onehot((_iota((L, L), 0) == owner_row) & ((block & 1) == j))


def places(tile_row, offset_row, put):
    tile = tile_row.astype(jnp.int32)
    offset = offset_row.astype(jnp.int32)
    start_row = (offset >> 7) * ROW_STEP + (tile & 15)
    line = _iota((L, L), 0)
    place = 2 * (_iota((L, L), 1) & 1)
    facts = jnp.where(
        line == place,
        start_row.astype(F32),
        jnp.where(line == place + 1, (offset & 127).astype(F32), 0.0),
    ).astype(BF16)
    return _dot_nt(put[0] + put[1], facts).astype(BF16)


def block_tables(tile_row, offset_row):
    owner = _owner(tile_row.astype(jnp.int32))
    shift = offset_row.astype(jnp.int32) & 127
    owner_col = _to_col(owner.astype(F32)).astype(jnp.int32)
    shift_col = _to_col(shift.astype(F32)).astype(jnp.int32)
    block = _iota((L, L), 0)
    device = _iota((L, L), 1)
    get = [_onehot((device == owner_col) & ((block & 1) == j)) for j in range(2)]
    put = [_blocks_of(owner, j) for j in range(2)]
    return get, put, jnp.broadcast_to(shift_col, (L, L))


def owner_tables(facts):
    facts = facts.astype(F32)
    pick, place, shifts = [], [], []
    for j in range(2):
        start_col = facts[:, 2 * j : 2 * j + 1]
        start_row = _to_row(start_col)
        for step in (0, ROW_STEP):
            pick.append(_onehot(_iota((L, L), 1).astype(F32) == start_col + step))
            place.append(_onehot(_iota((L, L), 0).astype(F32) == start_row + step))
        shifts.append(jnp.broadcast_to(facts[:, 2 * j + 1 : 2 * j + 2], (L, L)).astype(jnp.int32))
    return pick, place, shifts


def add_up(got, place, shifts):
    lane = _iota((L, L), 1)
    total = None
    for j in range(2):
        x = got[j].astype(F32)
        upper = jnp.where(lane >= shifts[j], x, 0.0).astype(BF16)
        lower = jnp.where(lane < shifts[j], x, 0.0).astype(BF16)
        part = _dot(place[2 * j], upper) + _dot(place[2 * j + 1], lower)
        total = part if total is None else total + part
    return total


def reply(field, pick, shifts):
    lane = _iota((L, L), 1)
    field = field.astype(BF16)
    return [
        jnp.where(
            lane >= shifts[j], _dot(pick[2 * j], field), _dot(pick[2 * j + 1], field)
        ).astype(BF16)
        for j in range(2)
    ]


def edge_row(field):
    lane = _iota((TILE, L), 1)
    tile = _iota((TILE, L), 0)
    first = field[0:TILE, 0:1]
    last = field[L - TILE : L, L - 1 : L]
    out = jnp.zeros((TILE, L), F32)
    for k, value in enumerate((first, last)):
        hi = value.astype(BF16).astype(F32)
        out = out + jnp.where(lane == tile + 32 * k, hi, 0.0)
        out = out + jnp.where(lane == tile + 32 * k + 16, value - hi, 0.0)
    return jnp.sum(out, axis=0, keepdims=True)


def outer_edges(edges, neighbours):
    lane = _iota((TILE, L), 1)
    found = []
    for side, base in ((0, 32), (1, 0)):
        line = neighbours[side : side + 1].astype(F32)
        own = _iota((TILE, TILE), 0) == _iota((TILE, TILE), 1)
        tile = jnp.sum(jnp.where(own, line, 0.0), axis=1, keepdims=True).astype(jnp.int32)
        rows = _dot(_onehot(lane == _owner(tile)), edges)
        at = base + (tile & 15)
        found.append(
            jnp.sum(jnp.where((lane == at) | (lane == at + 16), rows, 0.0), axis=1, keepdims=True)
        )
    return found


def prior(field, before, after):
    lane = _iota((L, L), 1)
    row = _iota((L, L), 0)
    to_right = _roll(field, 1, 1)
    to_left = _roll(field, L - 1, 1)
    left_in = _roll(to_right, ROW_STEP, 0)
    right_in = _roll(to_left, L - ROW_STEP, 0)
    pad = jnp.zeros((L - TILE, 1), F32)
    left_in = jnp.where(row < TILE, jnp.concatenate([before, pad], axis=0), left_in)
    right_in = jnp.where(row >= L - TILE, jnp.concatenate([pad, after], axis=0), right_in)
    lefts = jnp.where(lane == 0, left_in, to_right)
    rights = jnp.where(lane == L - 1, right_in, to_left)
    return smooth_weight * (2.0 * field - lefts - rights) + ridge_weight * field


def take_reply(got, get, shift):
    turned = _dot(get[0], got[0]) + _dot(get[1], got[1])
    return _rotate(turned.astype(BF16), ((L - shift) & 127).astype(jnp.int16)).astype(F32)


def send_back(back, put, shift):
    turned = _rotate(back.astype(BF16), shift.astype(jnp.int16))
    return [_dot(put[j], turned).astype(BF16) for j in range(2)]


CHUNK = 16
STEPS = (32, 48, 48)
DEPTH = 2


def rhs_kernel(
    tile_hbm, offset_hbm, tod_hbm, weight_hbm, beam_hbm,
    message_ref, normal_ref, get_ref, put_ref, shift_ref,
    tile_ref, offset_ref, tod_ref, weight_ref, beam_ref, weighted, back, scratch, small_sems, sems,
):
    small = [
        pltpu.make_async_copy(src, dst, small_sems.at[k])
        for k, (src, dst) in enumerate(
            (
                (tile_hbm, tile_ref),
                (offset_hbm, offset_ref),
                (tod_hbm, tod_ref),
                (weight_hbm, weight_ref),
            )
        )
    ]
    starts = [sum(STEPS[:k]) for k in range(len(STEPS))]
    beams = [
        pltpu.make_async_copy(
            beam_hbm.at[pl.ds(first, size)], beam_ref.at[pl.ds(first, size)], sems.at[k]
        )
        for k, (first, size) in enumerate(zip(starts, STEPS))
    ]

    for copy in small:
        copy.start()
    for copy in beams[:DEPTH]:
        copy.start()
    small[0].wait()
    small[1].wait()
    tile_row = _as_row(tile_ref[...], scratch)
    offset_row = _as_row(offset_ref[...], scratch)
    get, put, shift = block_tables(tile_row, offset_row)
    for j in range(2):
        get_ref[j] = get[j]
        put_ref[j] = put[j]
    shift_ref[...] = shift
    message_ref[2] = places(tile_row, offset_row, put)
    small[2].wait()
    small[3].wait()
    weighted[...] = (weight_ref[...] * tod_ref[...].astype(F32)).astype(BF16)
    row = _iota((CHUNK, FOOT), 0)

    for step, (start, size) in enumerate(zip(starts, STEPS)):
        beams[step].wait()
        if step + DEPTH < len(STEPS):
            beams[step + DEPTH].start()
        for first in range(start, start + size, CHUNK):
            rows = weighted[first : first + CHUNK]
            weight = weight_ref[first : first + CHUNK]
            out = jnp.zeros((CHUNK, FOOT), F32)
            for k in range(CHUNK):
                beam = beam_ref[first + k]
                turned = (beam.T.astype(F32) * weight[k : k + 1]).astype(BF16)
                found = _dot(jnp.concatenate([turned, rows], axis=0), beam)
                down, across = k % 2 * FOOT, k // 2 % 2 * FOOT
                normal_ref[(first + k) // 4, down : down + FOOT, across : across + FOOT] = found[
                    :FOOT
                ].astype(BF16)
                out = jnp.where(row == k, found[FOOT:], out)
            back[first : first + CHUNK] = out

    parts = send_back(back[...], put, shift)
    message_ref[0] = parts[0]
    message_ref[1] = parts[1]


def apply_normal(normal_ref, foot, back):
    row = _iota((CHUNK, FOOT), 0)
    for c in range(L // CHUNK):
        own = foot[c * CHUNK : (c + 1) * CHUNK]
        left = jnp.concatenate(
            [jnp.where((row & 1) == 0, own, 0.0), jnp.where((row & 1) == 1, own, 0.0)], axis=1
        ).astype(BF16)
        out = jnp.zeros((CHUNK, FOOT), F32)
        for q in range(CHUNK // 4):
            found = _dot(left, normal_ref[c * (CHUNK // 4) + q])
            out = jnp.where(
                (row >> 1) == 2 * q, found[:, :FOOT], jnp.where((row >> 1) == 2 * q + 1, found[:, FOOT:], out)
            )
        back[c * CHUNK : (c + 1) * CHUNK] = out
    return back[...]


def start_kernel(got_ref, field_ref, message_ref, pick_ref, place_ref, shift_ref):
    pick, place, shifts = owner_tables(got_ref[2])
    field = add_up((got_ref[0], got_ref[1]), place, shifts)
    replies = reply(field, pick, shifts)
    field_ref[...] = field
    message_ref[0] = replies[0]
    message_ref[1] = replies[1]
    message_ref[2] = jnp.broadcast_to(edge_row(field), (L, L)).astype(BF16)
    for k in range(4):
        pick_ref[k] = pick[k]
        place_ref[k] = place[k]
    for j in range(2):
        shift_ref[j] = shifts[j]


def first_apply_kernel(
    got_ref, get_ref, put_ref, shift_ref, normal_ref, message_ref, foot_ref, back
):
    shift = shift_ref[...]
    foot = take_reply((got_ref[0], got_ref[1]), (get_ref[0], get_ref[1]), shift)
    foot_ref[...] = foot
    parts = send_back(
        apply_normal(normal_ref, foot, back), (put_ref[0], put_ref[1]), shift
    )
    message_ref[0] = parts[0]
    message_ref[1] = parts[1]


def middle_kernel(got_ref, before_ref, field_ref, neighbour_ref, pick_ref, place_ref, shift_ref, image_ref, prior_ref, message_ref):
    field = field_ref[...]
    pick = [pick_ref[k] for k in range(4)]
    place = [place_ref[k] for k in range(4)]
    shifts = [shift_ref[j] for j in range(2)]
    before, after = outer_edges(before_ref[2], neighbour_ref[...])
    smooth = prior(field, before, after)
    image = add_up((got_ref[0], got_ref[1]), place, shifts) + smooth
    replies = reply(image, pick, shifts)
    prior_ref[...] = smooth
    image_ref[...] = image
    message_ref[0] = replies[0]
    message_ref[1] = replies[1]
    extra = (
        edge_row(image)
        + _pieces(_total(field * field), SCALARS)
        + _pieces(_total(field * image), SCALARS + 3)
    )
    message_ref[2] = jnp.broadcast_to(extra, (L, L)).astype(BF16)


def second_apply_kernel(
    got_ref, get_ref, put_ref, shift_ref, normal_ref, foot_ref, field_ref, image_ref, smooth_ref, neighbour_ref,
    message_ref, residual_ref, prior_ref, sums_ref, back,
):
    shift = shift_ref[...]
    sums = jnp.sum(got_ref[2].astype(F32), axis=0, keepdims=True)
    sums_ref[...] = sums
    step = _whole(sums, SCALARS) / _whole(sums, SCALARS + 3)
    taken = take_reply((got_ref[0], got_ref[1]), (get_ref[0], get_ref[1]), shift)
    foot = (foot_ref[...] - step * taken).astype(BF16).astype(F32)
    image = image_ref[...]
    before, after = outer_edges(got_ref[2], neighbour_ref[...])
    residual = field_ref[...] - step * image
    smooth = smooth_ref[...] - step * prior(image, before, after)
    residual_ref[...] = residual
    prior_ref[...] = smooth
    turned = apply_normal(normal_ref, foot, back)
    parts = send_back(turned, (put_ref[0], put_ref[1]), shift)
    message_ref[0] = parts[0]
    message_ref[1] = parts[1]
    square = _total(residual * residual)
    product = _total(foot * turned + residual * smooth)
    extra = _pieces(square, SCALARS) + _pieces(product, SCALARS + 3)
    message_ref[2] = jnp.broadcast_to(extra, (L, L)).astype(BF16)


def last_kernel(got_ref, place_ref, shift_ref, field_ref, image_ref, residual_ref, smooth_ref, sums_ref, solution_ref, rest_ref):
    place = [place_ref[k] for k in range(4)]
    shifts = [shift_ref[j] for j in range(2)]
    residual = residual_ref[...]
    field = field_ref[...]
    image = add_up((got_ref[0], got_ref[1]), place, shifts) + smooth_ref[...]
    sums = sums_ref[...]
    more = jnp.sum(got_ref[2].astype(F32), axis=0, keepdims=True)
    norm_first = _whole(sums, SCALARS)
    step_first = norm_first / _whole(sums, SCALARS + 3)
    norm = _whole(more, SCALARS)
    ratio = norm / norm_first
    step = norm / (_whole(more, SCALARS + 3) - ratio * norm / step_first)
    solution = step_first * field + step * (residual + ratio * field)
    rest = residual - step * (image + ratio * image_ref[...])
    for q in range(8):
        solution_ref[:, q * L : (q + 1) * L] = solution[q * TILE : (q + 1) * TILE]
        rest_ref[:, q * L : (q + 1) * L] = rest[q * TILE : (q + 1) * TILE]


def _shape(shape, dtype):
    return jax.ShapeDtypeStruct(shape, dtype)


def _full(shape):
    return pl.BlockSpec(shape, lambda g: (0,) * len(shape))


MAP = (L, L)
WIDE = _shape(MAP, F32)


def call(kernel, grid, in_specs, outs, out_specs, scratch, args, flops, size, vmem):
    return pl.pallas_call(
        kernel,
        grid=grid,
        in_specs=in_specs,
        out_specs=out_specs,
        out_shape=outs,
        scratch_shapes=scratch,
        compiler_params=pltpu.CompilerParams(vmem_limit_bytes=vmem * 2**20),
        cost_estimate=pl.CostEstimate(flops=flops, bytes_accessed=size, transcendentals=0),
    )(*args)


def whole_call(kernel, outs, args, scratch=(), flops=2**25, size=2**19):
    vmem = pl.BlockSpec(memory_space=pltpu.VMEM)
    return call(
        kernel, (), [vmem] * len(args), outs, [vmem] * len(outs), scratch, args, flops, size, 8
    )


def in_hbm(x):
    return pltpu.with_memory_space_constraint(x, pltpu.HBM)


def exchange(x):
    return lax.all_to_all(x, SEND, split_axis=1, concat_axis=1, tiled=True)


def per_device(tod, pointing, weights, tile_ids, offsets, neighbours):
    neighbours = neighbours.T

    message, normal, get, put, shift = call(
        rhs_kernel,
        (),
        [pl.BlockSpec(memory_space=pltpu.HBM)] * 5,
        [
            _shape((3, L, L), BF16),
            pltpu.VMEM((L // 4, 2 * FOOT, 2 * FOOT), BF16),
            _shape((2, L, L), BF16),
            _shape((2, L, L), BF16),
            _shape((L, L), jnp.int32),
        ],
        [pl.BlockSpec(memory_space=pltpu.VMEM)] * 5,
        [
            pltpu.VMEM(tile_ids.shape, jnp.int32),
            pltpu.VMEM(offsets.shape, jnp.int32),
            pltpu.VMEM((L, SAMP), BF16),
            pltpu.VMEM((L, SAMP), F32),
            pltpu.VMEM((L, SAMP, FOOT), BF16),
            pltpu.VMEM((L, SAMP), BF16),
            pltpu.VMEM((L, FOOT), F32),
            pltpu.VMEM((8, L), F32),
            pltpu.SemaphoreType.DMA((4,)),
            pltpu.SemaphoreType.DMA((len(STEPS),)),
        ],
        (
            in_hbm(tile_ids),
            in_hbm(offsets),
            in_hbm(tod.reshape(L, SAMP)),
            in_hbm(weights.reshape(L, SAMP)),
            in_hbm(pointing.reshape(L, SAMP, FOOT)),
        ),
        2**30,
        2**23,
        16,
    )
    got = exchange(message)

    field, message, pick, place, shifts = whole_call(
        start_kernel,
        [WIDE, _shape((3, L, L), BF16), _shape((4, L, L), BF16), _shape((4, L, L), BF16), _shape((2, L, L), jnp.int32)],
        (got,),
    )
    got_first = exchange(message)

    message, foot = whole_call(
        first_apply_kernel,
        [_shape((2, L, L), BF16), WIDE],
        (got_first, get, put, shift, normal),
        [pltpu.VMEM(MAP, F32)],
        2**28,
        2**22,
    )
    got = exchange(message)

    image, smooth, message = whole_call(
        middle_kernel,
        [WIDE, WIDE, _shape((3, L, L), BF16)],
        (got, got_first, field, neighbours, pick, place, shifts),
    )
    got = exchange(message)

    message, residual, smooth, sums = whole_call(
        second_apply_kernel,
        [_shape((3, L, L), BF16), WIDE, WIDE, _shape((1, L), F32)],
        (got, get, put, shift, normal, foot, field, image, smooth, neighbours),
        [pltpu.VMEM(MAP, F32)],
        2**28,
        2**22,
    )
    got = exchange(message)

    return tuple(
        whole_call(
            last_kernel,
            [_shape((TILE, 8 * L), F32)] * 2,
            (got, place, shifts, field, image, residual, smooth, sums),
        )
    )


def solution(mesh):
    split = Mesh(mesh.devices.reshape(mesh.shape["det"], 4, 4, 2), DET_TM)
    in_specs = (
        P("det", TM, None),
        P("det", TM, None, None),
        P("det", TM, None),
        P("det", TM),
        P("det", TM),
        P(DET_TM, None),
    )
    out_specs = (P(DET_TM, None), P(DET_TM, None))
    return jax.shard_map(
        per_device, mesh=split, in_specs=in_specs, out_specs=out_specs, check_vma=False
    )
```

```python
import jax
import jax.numpy as jnp
from jax import lax
from jax.experimental import pallas as pl
from jax.experimental.pallas import tpu as pltpu
from jax.sharding import Mesh
from jax.sharding import PartitionSpec as P


DET_TM = ("det", "tm_0", "tm_1", "tm_2")
TM = ("tm_0", "tm_1", "tm_2")
SEND = ("tm_2", "tm_1", "tm_0", "det")
SAMP = 256
FOOT = 128
L = 128
TILE = 16
ROW_STEP = 16
SCALARS = 64

smooth_weight = 2.0
ridge_weight = 0.5

F32 = jnp.float32
BF16 = jnp.bfloat16


def _roll(x, shift, axis):
    return pltpu.roll(x, shift, axis)


def _iota(shape, dim):
    return lax.broadcasted_iota(jnp.int32, shape, dim)


def _dot(a, b):
    return jnp.dot(a, b, preferred_element_type=F32)


def _dot_nt(a, b):
    return lax.dot_general(a, b, (((1,), (1,)), ((), ())), preferred_element_type=F32)


def _onehot(mask):
    return jnp.where(mask, 1.0, 0.0).astype(BF16)


def _to_col(row):
    eye = _iota((L, L), 0) == _iota((L, L), 1)
    return jnp.sum(jnp.where(eye, row, 0.0), axis=1, keepdims=True)


def _to_row(col):
    eye = _iota((L, L), 0) == _iota((L, L), 1)
    return jnp.sum(jnp.where(eye, col, 0.0), axis=0, keepdims=True)


def _rotate(x, amount):
    step = 1
    for base in (8, 4, 4):
        digit = (amount >> (step.bit_length() - 1)) & (base - 1)
        turned = x
        for value in range(1, base):
            turned = jnp.where(digit == value, _roll(x, step * value, 1), turned)
        x = turned
        step *= base
    return x


def _as_row(ids, scratch):
    scratch[...] = jnp.zeros(scratch.shape, F32)
    scratch[0:2, 0:64] = ids.astype(F32)
    x = scratch[...]
    return x[0:1] + _roll(x, 64, 1)[1:2]


def _pieces(value, first):
    hi = value.astype(BF16).astype(F32)
    mid = (value - hi).astype(BF16).astype(F32)
    lo = value - hi - mid
    lane = _iota((1, L), 1)
    return jnp.where(
        lane == first, hi, jnp.where(lane == first + 1, mid, jnp.where(lane == first + 2, lo, 0.0))
    )


def _whole(row, first):
    lane = _iota((1, L), 1)
    return jnp.sum(
        jnp.where((lane >= first) & (lane < first + 3), row, 0.0), axis=1, keepdims=True
    )


def _total(x):
    return jnp.sum(jnp.sum(x, axis=0, keepdims=True), axis=1, keepdims=True)


def _owner(tile):
    det, tm_0, tm_1, tm_2 = tile >> 9, (tile >> 7) & 3, (tile >> 5) & 3, (tile >> 4) & 1
    return (tm_2 << 6) | (tm_1 << 4) | (tm_0 << 2) | det


def _blocks_of(owner_row, j):
    block = _iota((L, L), 1)
    return _onehot((_iota((L, L), 0) == owner_row) & ((block & 1) == j))


def places(tile_row, offset_row, put):
    tile = tile_row.astype(jnp.int32)
    offset = offset_row.astype(jnp.int32)
    start_row = (offset >> 7) * ROW_STEP + (tile & 15)
    line = _iota((L, L), 0)
    place = 2 * (_iota((L, L), 1) & 1)
    facts = jnp.where(
        line == place,
        start_row.astype(F32),
        jnp.where(line == place + 1, (offset & 127).astype(F32), 0.0),
    ).astype(BF16)
    return _dot_nt(put[0] + put[1], facts).astype(BF16)


def block_tables(tile_row, offset_row):
    owner = _owner(tile_row.astype(jnp.int32))
    shift = offset_row.astype(jnp.int32) & 127
    owner_col = _to_col(owner.astype(F32)).astype(jnp.int32)
    shift_col = _to_col(shift.astype(F32)).astype(jnp.int32)
    block = _iota((L, L), 0)
    device = _iota((L, L), 1)
    get = [_onehot((device == owner_col) & ((block & 1) == j)) for j in range(2)]
    put = [_blocks_of(owner, j) for j in range(2)]
    return get, put, jnp.broadcast_to(shift_col, (L, L))


def owner_tables(facts):
    facts = facts.astype(F32)
    pick, place, shifts = [], [], []
    for j in range(2):
        start_col = facts[:, 2 * j : 2 * j + 1]
        start_row = _to_row(start_col)
        for step in (0, ROW_STEP):
            pick.append(_onehot(_iota((L, L), 1).astype(F32) == start_col + step))
            place.append(_onehot(_iota((L, L), 0).astype(F32) == start_row + step))
        shifts.append(jnp.broadcast_to(facts[:, 2 * j + 1 : 2 * j + 2], (L, L)).astype(jnp.int32))
    return pick, place, shifts


def add_up(got, place, shifts):
    lane = _iota((L, L), 1)
    total = None
    for j in range(2):
        x = got[j].astype(F32)
        upper = jnp.where(lane >= shifts[j], x, 0.0).astype(BF16)
        lower = jnp.where(lane < shifts[j], x, 0.0).astype(BF16)
        part = _dot(place[2 * j], upper) + _dot(place[2 * j + 1], lower)
        total = part if total is None else total + part
    return total


def reply(field, pick, shifts):
    lane = _iota((L, L), 1)
    field = field.astype(BF16)
    return [
        jnp.where(
            lane >= shifts[j], _dot(pick[2 * j], field), _dot(pick[2 * j + 1], field)
        ).astype(BF16)
        for j in range(2)
    ]


def edge_row(field):
    lane = _iota((TILE, L), 1)
    tile = _iota((TILE, L), 0)
    first = field[0:TILE, 0:1]
    last = field[L - TILE : L, L - 1 : L]
    out = jnp.zeros((TILE, L), F32)
    for k, value in enumerate((first, last)):
        hi = value.astype(BF16).astype(F32)
        out = out + jnp.where(lane == tile + 32 * k, hi, 0.0)
        out = out + jnp.where(lane == tile + 32 * k + 16, value - hi, 0.0)
    return jnp.sum(out, axis=0, keepdims=True)


def outer_edges(edges, neighbours):
    lane = _iota((TILE, L), 1)
    found = []
    for side, base in ((0, 32), (1, 0)):
        line = neighbours[side : side + 1].astype(F32)
        own = _iota((TILE, TILE), 0) == _iota((TILE, TILE), 1)
        tile = jnp.sum(jnp.where(own, line, 0.0), axis=1, keepdims=True).astype(jnp.int32)
        rows = _dot(_onehot(lane == _owner(tile)), edges)
        at = base + (tile & 15)
        found.append(
            jnp.sum(jnp.where((lane == at) | (lane == at + 16), rows, 0.0), axis=1, keepdims=True)
        )
    return found


def prior(field, before, after):
    lane = _iota((L, L), 1)
    row = _iota((L, L), 0)
    to_right = _roll(field, 1, 1)
    to_left = _roll(field, L - 1, 1)
    left_in = _roll(to_right, ROW_STEP, 0)
    right_in = _roll(to_left, L - ROW_STEP, 0)
    pad = jnp.zeros((L - TILE, 1), F32)
    left_in = jnp.where(row < TILE, jnp.concatenate([before, pad], axis=0), left_in)
    right_in = jnp.where(row >= L - TILE, jnp.concatenate([pad, after], axis=0), right_in)
    lefts = jnp.where(lane == 0, left_in, to_right)
    rights = jnp.where(lane == L - 1, right_in, to_left)
    return smooth_weight * (2.0 * field - lefts - rights) + ridge_weight * field


def take_reply(got, get, shift):
    turned = _dot(get[0], got[0]) + _dot(get[1], got[1])
    return _rotate(turned.astype(BF16), ((L - shift) & 127).astype(jnp.int16)).astype(F32)


def send_back(back, put, shift):
    turned = _rotate(back.astype(BF16), shift.astype(jnp.int16))
    return [_dot(put[j], turned).astype(BF16) for j in range(2)]


CHUNK = 16
STEPS = (32, 48, 48)
DEPTH = 2


def rhs_kernel(
    tile_hbm, offset_hbm, tod_hbm, weight_hbm, beam_hbm,
    message_ref, normal_ref, get_ref, put_ref, shift_ref,
    tile_ref, offset_ref, tod_ref, weight_ref, beam_ref, weighted, back, scratch, small_sems, sems,
):
    small = [
        pltpu.make_async_copy(src, dst, small_sems.at[k])
        for k, (src, dst) in enumerate(
            (
                (tile_hbm, tile_ref),
                (offset_hbm, offset_ref),
                (tod_hbm, tod_ref),
                (weight_hbm, weight_ref),
            )
        )
    ]
    starts = [sum(STEPS[:k]) for k in range(len(STEPS))]
    beams = [
        pltpu.make_async_copy(
            beam_hbm.at[pl.ds(first, size)], beam_ref.at[pl.ds(first, size)], sems.at[k]
        )
        for k, (first, size) in enumerate(zip(starts, STEPS))
    ]

    for copy in small:
        copy.start()
    for copy in beams[:DEPTH]:
        copy.start()
    small[0].wait()
    small[1].wait()
    tile_row = _as_row(tile_ref[...], scratch)
    offset_row = _as_row(offset_ref[...], scratch)
    get, put, shift = block_tables(tile_row, offset_row)
    for j in range(2):
        get_ref[j] = get[j]
        put_ref[j] = put[j]
    shift_ref[...] = shift
    message_ref[2] = places(tile_row, offset_row, put)
    small[2].wait()
    small[3].wait()
    weighted[...] = (weight_ref[...] * tod_ref[...].astype(F32)).astype(BF16)
    row = _iota((CHUNK, FOOT), 0)

    for step, (start, size) in enumerate(zip(starts, STEPS)):
        beams[step].wait()
        if step + DEPTH < len(STEPS):
            beams[step + DEPTH].start()
        for first in range(start, start + size, CHUNK):
            rows = weighted[first : first + CHUNK]
            weight = weight_ref[first : first + CHUNK]
            out = jnp.zeros((CHUNK, FOOT), F32)
            for k in range(CHUNK):
                beam = beam_ref[first + k]
                turned = (beam.T.astype(F32) * weight[k : k + 1]).astype(BF16)
                found = _dot(jnp.concatenate([turned, rows], axis=0), beam)
                down, across = k % 2 * FOOT, k // 2 % 2 * FOOT
                normal_ref[(first + k) // 4, down : down + FOOT, across : across + FOOT] = found[
                    :FOOT
                ].astype(BF16)
                out = jnp.where(row == k, found[FOOT:], out)
            back[first : first + CHUNK] = out

    parts = send_back(back[...], put, shift)
    message_ref[0] = parts[0]
    message_ref[1] = parts[1]


def apply_normal(normal_ref, foot, back):
    row = _iota((CHUNK, FOOT), 0)
    for c in range(L // CHUNK):
        own = foot[c * CHUNK : (c + 1) * CHUNK]
        left = jnp.concatenate(
            [jnp.where((row & 1) == 0, own, 0.0), jnp.where((row & 1) == 1, own, 0.0)], axis=1
        ).astype(BF16)
        out = jnp.zeros((CHUNK, FOOT), F32)
        for q in range(CHUNK // 4):
            found = _dot(left, normal_ref[c * (CHUNK // 4) + q])
            out = jnp.where(
                (row >> 1) == 2 * q, found[:, :FOOT], jnp.where((row >> 1) == 2 * q + 1, found[:, FOOT:], out)
            )
        back[c * CHUNK : (c + 1) * CHUNK] = out
    return back[...]


def start_kernel(got_ref, field_ref, message_ref, pick_ref, place_ref, shift_ref):
    pick, place, shifts = owner_tables(got_ref[2])
    field = add_up((got_ref[0], got_ref[1]), place, shifts)
    replies = reply(field, pick, shifts)
    field_ref[...] = field
    message_ref[0] = replies[0]
    message_ref[1] = replies[1]
    message_ref[2] = jnp.broadcast_to(edge_row(field), (L, L)).astype(BF16)
    for k in range(4):
        pick_ref[k] = pick[k]
        place_ref[k] = place[k]
    for j in range(2):
        shift_ref[j] = shifts[j]


def first_apply_kernel(
    got_ref, get_ref, put_ref, shift_ref, normal_ref, field_ref, neighbour_ref, message_ref, foot_ref, prior_ref, back
):
    shift = shift_ref[...]
    foot = take_reply((got_ref[0], got_ref[1]), (get_ref[0], get_ref[1]), shift)
    foot_ref[...] = foot
    parts = send_back(
        apply_normal(normal_ref, foot, back), (put_ref[0], put_ref[1]), shift
    )
    message_ref[0] = parts[0]
    message_ref[1] = parts[1]
    before, after = outer_edges(got_ref[2], neighbour_ref[...])
    prior_ref[...] = prior(field_ref[...], before, after)


def middle_kernel(got_ref, field_ref, smooth_ref, pick_ref, place_ref, shift_ref, image_ref, message_ref):
    field = field_ref[...]
    pick = [pick_ref[k] for k in range(4)]
    place = [place_ref[k] for k in range(4)]
    shifts = [shift_ref[j] for j in range(2)]
    image = add_up((got_ref[0], got_ref[1]), place, shifts) + smooth_ref[...]
    replies = reply(image, pick, shifts)
    image_ref[...] = image
    message_ref[0] = replies[0]
    message_ref[1] = replies[1]
    extra = (
        edge_row(image)
        + _pieces(_total(field * field), SCALARS)
        + _pieces(_total(field * image), SCALARS + 3)
    )
    message_ref[2] = jnp.broadcast_to(extra, (L, L)).astype(BF16)


def second_apply_kernel(
    got_ref, get_ref, put_ref, shift_ref, normal_ref, foot_ref, field_ref, image_ref, smooth_ref, neighbour_ref,
    message_ref, residual_ref, prior_ref, sums_ref, back,
):
    shift = shift_ref[...]
    sums = jnp.sum(got_ref[2].astype(F32), axis=0, keepdims=True)
    sums_ref[...] = sums
    step = _whole(sums, SCALARS) / _whole(sums, SCALARS + 3)
    taken = take_reply((got_ref[0], got_ref[1]), (get_ref[0], get_ref[1]), shift)
    foot = (foot_ref[...] - step * taken).astype(BF16).astype(F32)
    image = image_ref[...]
    before, after = outer_edges(got_ref[2], neighbour_ref[...])
    residual = field_ref[...] - step * image
    smooth = smooth_ref[...] - step * prior(image, before, after)
    residual_ref[...] = residual
    prior_ref[...] = smooth
    turned = apply_normal(normal_ref, foot, back)
    parts = send_back(turned, (put_ref[0], put_ref[1]), shift)
    message_ref[0] = parts[0]
    message_ref[1] = parts[1]
    square = _total(residual * residual)
    product = _total(foot * turned + residual * smooth)
    extra = _pieces(square, SCALARS) + _pieces(product, SCALARS + 3)
    message_ref[2] = jnp.broadcast_to(extra, (L, L)).astype(BF16)


def last_kernel(got_ref, place_ref, shift_ref, field_ref, image_ref, residual_ref, smooth_ref, sums_ref, solution_ref, rest_ref):
    place = [place_ref[k] for k in range(4)]
    shifts = [shift_ref[j] for j in range(2)]
    residual = residual_ref[...]
    field = field_ref[...]
    image = add_up((got_ref[0], got_ref[1]), place, shifts) + smooth_ref[...]
    sums = sums_ref[...]
    more = jnp.sum(got_ref[2].astype(F32), axis=0, keepdims=True)
    norm_first = _whole(sums, SCALARS)
    step_first = norm_first / _whole(sums, SCALARS + 3)
    norm = _whole(more, SCALARS)
    ratio = norm / norm_first
    step = norm / (_whole(more, SCALARS + 3) - ratio * norm / step_first)
    solution = step_first * field + step * (residual + ratio * field)
    rest = residual - step * (image + ratio * image_ref[...])
    for q in range(8):
        solution_ref[:, q * L : (q + 1) * L] = solution[q * TILE : (q + 1) * TILE]
        rest_ref[:, q * L : (q + 1) * L] = rest[q * TILE : (q + 1) * TILE]


def _shape(shape, dtype):
    return jax.ShapeDtypeStruct(shape, dtype)


def _full(shape):
    return pl.BlockSpec(shape, lambda g: (0,) * len(shape))


MAP = (L, L)
WIDE = _shape(MAP, F32)


def call(kernel, grid, in_specs, outs, out_specs, scratch, args, flops, size, vmem):
    return pl.pallas_call(
        kernel,
        grid=grid,
        in_specs=in_specs,
        out_specs=out_specs,
        out_shape=outs,
        scratch_shapes=scratch,
        compiler_params=pltpu.CompilerParams(vmem_limit_bytes=vmem * 2**20),
        cost_estimate=pl.CostEstimate(flops=flops, bytes_accessed=size, transcendentals=0),
    )(*args)


def whole_call(kernel, outs, args, scratch=(), flops=2**25, size=2**19):
    vmem = pl.BlockSpec(memory_space=pltpu.VMEM)
    return call(
        kernel, (), [vmem] * len(args), outs, [vmem] * len(outs), scratch, args, flops, size, 8
    )


def in_hbm(x):
    return pltpu.with_memory_space_constraint(x, pltpu.HBM)


def exchange(x):
    return lax.all_to_all(x, SEND, split_axis=1, concat_axis=1, tiled=True)


def per_device(tod, pointing, weights, tile_ids, offsets, neighbours):
    neighbours = neighbours.T

    message, normal, get, put, shift = call(
        rhs_kernel,
        (),
        [pl.BlockSpec(memory_space=pltpu.HBM)] * 5,
        [
            _shape((3, L, L), BF16),
            pltpu.VMEM((L // 4, 2 * FOOT, 2 * FOOT), BF16),
            _shape((2, L, L), BF16),
            _shape((2, L, L), BF16),
            _shape((L, L), jnp.int32),
        ],
        [pl.BlockSpec(memory_space=pltpu.VMEM)] * 5,
        [
            pltpu.VMEM(tile_ids.shape, jnp.int32),
            pltpu.VMEM(offsets.shape, jnp.int32),
            pltpu.VMEM((L, SAMP), BF16),
            pltpu.VMEM((L, SAMP), F32),
            pltpu.VMEM((L, SAMP, FOOT), BF16),
            pltpu.VMEM((L, SAMP), BF16),
            pltpu.VMEM((L, FOOT), F32),
            pltpu.VMEM((8, L), F32),
            pltpu.SemaphoreType.DMA((4,)),
            pltpu.SemaphoreType.DMA((len(STEPS),)),
        ],
        (
            in_hbm(tile_ids),
            in_hbm(offsets),
            in_hbm(tod.reshape(L, SAMP)),
            in_hbm(weights.reshape(L, SAMP)),
            in_hbm(pointing.reshape(L, SAMP, FOOT)),
        ),
        2**30,
        2**23,
        16,
    )
    got = exchange(message)

    field, message, pick, place, shifts = whole_call(
        start_kernel,
        [WIDE, _shape((3, L, L), BF16), _shape((4, L, L), BF16), _shape((4, L, L), BF16), _shape((2, L, L), jnp.int32)],
        (got,),
    )
    got = exchange(message)

    message, foot, smooth = whole_call(
        first_apply_kernel,
        [_shape((2, L, L), BF16), WIDE, WIDE],
        (got, get, put, shift, normal, field, neighbours),
        [pltpu.VMEM(MAP, F32)],
        2**28,
        2**22,
    )
    got = exchange(message)

    image, message = whole_call(
        middle_kernel,
        [WIDE, _shape((3, L, L), BF16)],
        (got, field, smooth, pick, place, shifts),
    )
    got = exchange(message)

    message, residual, smooth, sums = whole_call(
        second_apply_kernel,
        [_shape((3, L, L), BF16), WIDE, WIDE, _shape((1, L), F32)],
        (got, get, put, shift, normal, foot, field, image, smooth, neighbours),
        [pltpu.VMEM(MAP, F32)],
        2**28,
        2**22,
    )
    got = exchange(message)

    return tuple(
        whole_call(
            last_kernel,
            [_shape((TILE, 8 * L), F32)] * 2,
            (got, place, shifts, field, image, residual, smooth, sums),
        )
    )


def solution(mesh):
    split = Mesh(mesh.devices.reshape(mesh.shape["det"], 4, 4, 2), DET_TM)
    in_specs = (
        P("det", TM, None),
        P("det", TM, None, None),
        P("det", TM, None),
        P("det", TM),
        P("det", TM),
        P(DET_TM, None),
    )
    out_specs = (P(DET_TM, None), P(DET_TM, None))
    return jax.shard_map(
        per_device, mesh=split, in_specs=in_specs, out_specs=out_specs, check_vma=False
    )
```

```python
import jax
import jax.numpy as jnp
from jax import lax
from jax.experimental import pallas as pl
from jax.experimental.pallas import tpu as pltpu
from jax.sharding import Mesh
from jax.sharding import PartitionSpec as P


DET_TM = ("det", "tm_0", "tm_1", "tm_2")
TM = ("tm_0", "tm_1", "tm_2")
SEND = ("tm_2", "tm_1", "tm_0", "det")
SAMP = 256
FOOT = 128
L = 128
TILE = 16
ROW_STEP = 16
SCALARS = 64

smooth_weight = 2.0
ridge_weight = 0.5

F32 = jnp.float32
BF16 = jnp.bfloat16


def _roll(x, shift, axis):
    return pltpu.roll(x, shift, axis)


def _iota(shape, dim):
    return lax.broadcasted_iota(jnp.int32, shape, dim)


def _dot(a, b):
    return jnp.dot(a, b, preferred_element_type=F32)


def _dot_nt(a, b):
    return lax.dot_general(a, b, (((1,), (1,)), ((), ())), preferred_element_type=F32)


def _onehot(mask):
    return jnp.where(mask, 1.0, 0.0).astype(BF16)


def _to_col(row):
    eye = _iota((L, L), 0) == _iota((L, L), 1)
    return jnp.sum(jnp.where(eye, row, 0.0), axis=1, keepdims=True)


def _to_row(col):
    eye = _iota((L, L), 0) == _iota((L, L), 1)
    return jnp.sum(jnp.where(eye, col, 0.0), axis=0, keepdims=True)


def _rotate(x, amount):
    step = 1
    for base in (8, 4, 4):
        digit = (amount >> (step.bit_length() - 1)) & (base - 1)
        turned = x
        for value in range(1, base):
            turned = jnp.where(digit == value, _roll(x, step * value, 1), turned)
        x = turned
        step *= base
    return x


def _as_row(ids, scratch):
    scratch[...] = jnp.zeros(scratch.shape, F32)
    scratch[0:2, 0:64] = ids.astype(F32)
    x = scratch[...]
    return x[0:1] + _roll(x, 64, 1)[1:2]


def _pieces(value, first):
    hi = value.astype(BF16).astype(F32)
    mid = (value - hi).astype(BF16).astype(F32)
    lo = value - hi - mid
    lane = _iota((1, L), 1)
    return jnp.where(
        lane == first, hi, jnp.where(lane == first + 1, mid, jnp.where(lane == first + 2, lo, 0.0))
    )


def _whole(row, first):
    lane = _iota((1, L), 1)
    return jnp.sum(
        jnp.where((lane >= first) & (lane < first + 3), row, 0.0), axis=1, keepdims=True
    )


def _total(x):
    return jnp.sum(jnp.sum(x, axis=0, keepdims=True), axis=1, keepdims=True)


def _owner(tile):
    det, tm_0, tm_1, tm_2 = tile >> 9, (tile >> 7) & 3, (tile >> 5) & 3, (tile >> 4) & 1
    return (tm_2 << 6) | (tm_1 << 4) | (tm_0 << 2) | det


def _blocks_of(owner_row, rows):
    line = _iota((L * rows, L), 0)
    return _onehot(line == owner_row * rows + (_iota((L * rows, L), 1) & 1))


def places(tile_row, offset_row):
    tile = tile_row.astype(jnp.int32)
    offset = offset_row.astype(jnp.int32)
    start_row = (offset >> 7) * ROW_STEP + (tile & 15)
    line = _iota((L, L), 0)
    place = 2 * (_iota((L, L), 1) & 1)
    facts = jnp.where(
        line == place,
        start_row.astype(F32),
        jnp.where(line == place + 1, (offset & 127).astype(F32), 0.0),
    ).astype(BF16)
    third = _onehot(_iota((4 * L, L), 0) == _owner(tile) * 4 + 2)
    return _dot_nt(third, facts)


def block_tables(tile_row, offset_row):
    owner = _owner(tile_row.astype(jnp.int32))
    shift = offset_row.astype(jnp.int32) & 127
    owner_col = _to_col(owner.astype(F32)).astype(jnp.int32)
    shift_col = _to_col(shift.astype(F32)).astype(jnp.int32)
    block = _iota((L, L), 0)
    device = _iota((L, L), 1)
    get = [_onehot((device == owner_col) & ((block & 1) == j)) for j in range(2)]
    return get, _blocks_of(owner, 2), _blocks_of(owner, 4), jnp.broadcast_to(shift_col, (L, L))


def owner_tables(facts):
    facts = facts.astype(F32)
    pick, place, shifts = [], [], []
    for j in range(2):
        start_col = facts[:, 2 * j : 2 * j + 1]
        start_row = _to_row(start_col)
        for step in (0, ROW_STEP):
            pick.append(_onehot(_iota((L, L), 1).astype(F32) == start_col + step))
            place.append(_onehot(_iota((L, L), 0).astype(F32) == start_row + step))
        shifts.append(jnp.broadcast_to(facts[:, 2 * j + 1 : 2 * j + 2], (L, L)).astype(jnp.int32))
    return pick, place, shifts


def add_up(got, place, shifts):
    lane = _iota((L, L), 1)
    total = None
    for j in range(2):
        x = got[j].astype(F32)
        upper = jnp.where(lane >= shifts[j], x, 0.0).astype(BF16)
        lower = jnp.where(lane < shifts[j], x, 0.0).astype(BF16)
        part = _dot(place[2 * j], upper) + _dot(place[2 * j + 1], lower)
        total = part if total is None else total + part
    return total


def reply(field, pick, shifts):
    lane = _iota((L, L), 1)
    field = field.astype(BF16)
    return [
        jnp.where(
            lane >= shifts[j], _dot(pick[2 * j], field), _dot(pick[2 * j + 1], field)
        ).astype(BF16)
        for j in range(2)
    ]


def edge_row(field):
    lane = _iota((TILE, L), 1)
    tile = _iota((TILE, L), 0)
    first = field[0:TILE, 0:1]
    last = field[L - TILE : L, L - 1 : L]
    out = jnp.zeros((TILE, L), F32)
    for k, value in enumerate((first, last)):
        hi = value.astype(BF16).astype(F32)
        out = out + jnp.where(lane == tile + 32 * k, hi, 0.0)
        out = out + jnp.where(lane == tile + 32 * k + 16, value - hi, 0.0)
    return jnp.sum(out, axis=0, keepdims=True)


def outer_edges(edges, neighbours):
    lane = _iota((TILE, L), 1)
    found = []
    for side, base in ((0, 32), (1, 0)):
        line = neighbours[side : side + 1].astype(F32)
        own = _iota((TILE, TILE), 0) == _iota((TILE, TILE), 1)
        tile = jnp.sum(jnp.where(own, line, 0.0), axis=1, keepdims=True).astype(jnp.int32)
        rows = _dot(_onehot(lane == _owner(tile)), edges)
        at = base + (tile & 15)
        found.append(
            jnp.sum(jnp.where((lane == at) | (lane == at + 16), rows, 0.0), axis=1, keepdims=True)
        )
    return found


def prior(field, before, after):
    lane = _iota((L, L), 1)
    row = _iota((L, L), 0)
    to_right = _roll(field, 1, 1)
    to_left = _roll(field, L - 1, 1)
    left_in = _roll(to_right, ROW_STEP, 0)
    right_in = _roll(to_left, L - ROW_STEP, 0)
    pad = jnp.zeros((L - TILE, 1), F32)
    left_in = jnp.where(row < TILE, jnp.concatenate([before, pad], axis=0), left_in)
    right_in = jnp.where(row >= L - TILE, jnp.concatenate([pad, after], axis=0), right_in)
    lefts = jnp.where(lane == 0, left_in, to_right)
    rights = jnp.where(lane == L - 1, right_in, to_left)
    return smooth_weight * (2.0 * field - lefts - rights) + ridge_weight * field


def take_reply(got, get, shift):
    turned = _dot(get[0], got[0]) + _dot(get[1], got[1])
    return _rotate(turned.astype(BF16), ((L - shift) & 127).astype(jnp.int16)).astype(F32)


def send_back(back, put, shift):
    turned = _rotate(back.astype(BF16), shift.astype(jnp.int16))
    return _dot(put, turned)


CHUNK = 16
STEPS = (32, 48, 48)
DEPTH = 2


def rhs_kernel(
    tile_hbm, offset_hbm, tod_hbm, weight_hbm, beam_hbm,
    message_ref, normal_ref, get_ref, put_2_ref, put_4_ref, shift_ref,
    tile_ref, offset_ref, tod_ref, weight_ref, beam_ref, weighted, back, scratch, facts, small_sems, sems,
):
    small = [
        pltpu.make_async_copy(src, dst, small_sems.at[k])
        for k, (src, dst) in enumerate(
            (
                (tile_hbm, tile_ref),
                (offset_hbm, offset_ref),
                (tod_hbm, tod_ref),
                (weight_hbm, weight_ref),
            )
        )
    ]
    starts = [sum(STEPS[:k]) for k in range(len(STEPS))]
    beams = [
        pltpu.make_async_copy(
            beam_hbm.at[pl.ds(first, size)], beam_ref.at[pl.ds(first, size)], sems.at[k]
        )
        for k, (first, size) in enumerate(zip(starts, STEPS))
    ]

    for copy in small:
        copy.start()
    for copy in beams[:DEPTH]:
        copy.start()
    small[0].wait()
    small[1].wait()
    tile_row = _as_row(tile_ref[...], scratch)
    offset_row = _as_row(offset_ref[...], scratch)
    get, put_2, put_4, shift = block_tables(tile_row, offset_row)
    for j in range(2):
        get_ref[j] = get[j]
    put_2_ref[...] = put_2
    put_4_ref[...] = put_4
    shift_ref[...] = shift
    facts[...] = places(tile_row, offset_row)
    small[2].wait()
    small[3].wait()
    weighted[...] = (weight_ref[...] * tod_ref[...].astype(F32)).astype(BF16)
    row = _iota((CHUNK, FOOT), 0)

    for step, (start, size) in enumerate(zip(starts, STEPS)):
        beams[step].wait()
        if step + DEPTH < len(STEPS):
            beams[step + DEPTH].start()
        for first in range(start, start + size, CHUNK):
            rows = weighted[first : first + CHUNK]
            weight = weight_ref[first : first + CHUNK]
            out = jnp.zeros((CHUNK, FOOT), F32)
            for k in range(CHUNK):
                beam = beam_ref[first + k]
                turned = (beam.T.astype(F32) * weight[k : k + 1]).astype(BF16)
                found = _dot(jnp.concatenate([turned, rows], axis=0), beam)
                down, across = k % 2 * FOOT, k // 2 % 2 * FOOT
                normal_ref[(first + k) // 4, down : down + FOOT, across : across + FOOT] = found[
                    :FOOT
                ].astype(BF16)
                out = jnp.where(row == k, found[FOOT:], out)
            back[first : first + CHUNK] = out

    message_ref[...] = (facts[...] + send_back(back[...], put_4_ref[...], shift_ref[...])).astype(BF16)


def apply_normal(normal_ref, foot, back):
    row = _iota((CHUNK, FOOT), 0)
    for c in range(L // CHUNK):
        own = foot[c * CHUNK : (c + 1) * CHUNK]
        left = jnp.concatenate(
            [jnp.where((row & 1) == 0, own, 0.0), jnp.where((row & 1) == 1, own, 0.0)], axis=1
        ).astype(BF16)
        out = jnp.zeros((CHUNK, FOOT), F32)
        for q in range(CHUNK // 4):
            found = _dot(left, normal_ref[c * (CHUNK // 4) + q])
            out = jnp.where(
                (row >> 1) == 2 * q, found[:, :FOOT], jnp.where((row >> 1) == 2 * q + 1, found[:, FOOT:], out)
            )
        back[c * CHUNK : (c + 1) * CHUNK] = out
    return back[...]


def start_kernel(got_ref, field_ref, message_ref, pick_ref, place_ref, shift_ref):
    pick, place, shifts = owner_tables(got_ref[2])
    field = add_up((got_ref[0], got_ref[1]), place, shifts)
    replies = reply(field, pick, shifts)
    field_ref[...] = field
    message_ref[0] = replies[0]
    message_ref[1] = replies[1]
    message_ref[2] = jnp.broadcast_to(edge_row(field), (L, L)).astype(BF16)
    for k in range(4):
        pick_ref[k] = pick[k]
        place_ref[k] = place[k]
    for j in range(2):
        shift_ref[j] = shifts[j]


def first_apply_kernel(
    got_ref, get_ref, put_ref, shift_ref, normal_ref, field_ref, neighbour_ref, message_ref, foot_ref, prior_ref, back
):
    shift = shift_ref[...]
    foot = take_reply((got_ref[0], got_ref[1]), (get_ref[0], get_ref[1]), shift)
    foot_ref[...] = foot
    turned = apply_normal(normal_ref, foot, back)
    message_ref[...] = send_back(turned, put_ref[...], shift).astype(BF16)
    before, after = outer_edges(got_ref[2], neighbour_ref[...])
    prior_ref[...] = prior(field_ref[...], before, after)


def middle_kernel(got_ref, field_ref, smooth_ref, pick_ref, place_ref, shift_ref, image_ref, message_ref):
    field = field_ref[...]
    pick = [pick_ref[k] for k in range(4)]
    place = [place_ref[k] for k in range(4)]
    shifts = [shift_ref[j] for j in range(2)]
    image = add_up((got_ref[0], got_ref[1]), place, shifts) + smooth_ref[...]
    replies = reply(image, pick, shifts)
    image_ref[...] = image
    message_ref[0] = replies[0]
    message_ref[1] = replies[1]
    extra = (
        edge_row(image)
        + _pieces(_total(field * field), SCALARS)
        + _pieces(_total(field * image), SCALARS + 3)
    )
    message_ref[2] = jnp.broadcast_to(extra, (L, L)).astype(BF16)


def second_apply_kernel(
    got_ref, get_ref, put_ref, shift_ref, normal_ref, foot_ref, field_ref, image_ref, smooth_ref, neighbour_ref,
    message_ref, residual_ref, prior_ref, sums_ref, back,
):
    shift = shift_ref[...]
    sums = jnp.sum(got_ref[2].astype(F32), axis=0, keepdims=True)
    sums_ref[...] = sums
    step = _whole(sums, SCALARS) / _whole(sums, SCALARS + 3)
    taken = take_reply((got_ref[0], got_ref[1]), (get_ref[0], get_ref[1]), shift)
    foot = (foot_ref[...] - step * taken).astype(BF16).astype(F32)
    image = image_ref[...]
    before, after = outer_edges(got_ref[2], neighbour_ref[...])
    residual = field_ref[...] - step * image
    smooth = smooth_ref[...] - step * prior(image, before, after)
    residual_ref[...] = residual
    prior_ref[...] = smooth
    turned = apply_normal(normal_ref, foot, back)
    square = _total(residual * residual)
    product = _total(foot * turned + residual * smooth)
    extra = _pieces(square, SCALARS) + _pieces(product, SCALARS + 3)
    third = (_iota((4 * L, L), 0) & 3) == 2
    message_ref[...] = jnp.where(third, extra, send_back(turned, put_ref[...], shift)).astype(BF16)


def last_kernel(got_ref, place_ref, shift_ref, field_ref, image_ref, residual_ref, smooth_ref, sums_ref, solution_ref, rest_ref):
    place = [place_ref[k] for k in range(4)]
    shifts = [shift_ref[j] for j in range(2)]
    residual = residual_ref[...]
    field = field_ref[...]
    image = add_up((got_ref[0], got_ref[1]), place, shifts) + smooth_ref[...]
    sums = sums_ref[...]
    more = jnp.sum(got_ref[2].astype(F32), axis=0, keepdims=True)
    norm_first = _whole(sums, SCALARS)
    step_first = norm_first / _whole(sums, SCALARS + 3)
    norm = _whole(more, SCALARS)
    ratio = norm / norm_first
    step = norm / (_whole(more, SCALARS + 3) - ratio * norm / step_first)
    solution = step_first * field + step * (residual + ratio * field)
    rest = residual - step * (image + ratio * image_ref[...])
    for q in range(8):
        solution_ref[:, q * L : (q + 1) * L] = solution[q * TILE : (q + 1) * TILE]
        rest_ref[:, q * L : (q + 1) * L] = rest[q * TILE : (q + 1) * TILE]


def _shape(shape, dtype):
    return jax.ShapeDtypeStruct(shape, dtype)


def _full(shape):
    return pl.BlockSpec(shape, lambda g: (0,) * len(shape))


MAP = (L, L)
WIDE = _shape(MAP, F32)


def call(kernel, grid, in_specs, outs, out_specs, scratch, args, flops, size, vmem):
    return pl.pallas_call(
        kernel,
        grid=grid,
        in_specs=in_specs,
        out_specs=out_specs,
        out_shape=outs,
        scratch_shapes=scratch,
        compiler_params=pltpu.CompilerParams(vmem_limit_bytes=vmem * 2**20),
        cost_estimate=pl.CostEstimate(flops=flops, bytes_accessed=size, transcendentals=0),
    )(*args)


def whole_call(kernel, outs, args, scratch=(), flops=2**25, size=2**19):
    vmem = pl.BlockSpec(memory_space=pltpu.VMEM)
    return call(
        kernel, (), [vmem] * len(args), outs, [vmem] * len(outs), scratch, args, flops, size, 8
    )


def in_hbm(x):
    return pltpu.with_memory_space_constraint(x, pltpu.HBM)


def exchange(x):
    return lax.all_to_all(x, SEND, split_axis=1, concat_axis=1, tiled=True)


def exchange_rows(x):
    x = lax.all_to_all(x.reshape(L, -1, L), SEND, split_axis=0, concat_axis=0, tiled=True)
    return x.transpose(1, 0, 2)


def per_device(tod, pointing, weights, tile_ids, offsets, neighbours):
    neighbours = neighbours.T

    message, normal, get, put_2, put_4, shift = call(
        rhs_kernel,
        (),
        [pl.BlockSpec(memory_space=pltpu.HBM)] * 5,
        [
            _shape((4 * L, L), BF16),
            pltpu.VMEM((L // 4, 2 * FOOT, 2 * FOOT), BF16),
            _shape((2, L, L), BF16),
            _shape((2 * L, L), BF16),
            _shape((4 * L, L), BF16),
            _shape((L, L), jnp.int32),
        ],
        [pl.BlockSpec(memory_space=pltpu.VMEM)] * 6,
        [
            pltpu.VMEM(tile_ids.shape, jnp.int32),
            pltpu.VMEM(offsets.shape, jnp.int32),
            pltpu.VMEM((L, SAMP), BF16),
            pltpu.VMEM((L, SAMP), F32),
            pltpu.VMEM((L, SAMP, FOOT), BF16),
            pltpu.VMEM((L, SAMP), BF16),
            pltpu.VMEM((L, FOOT), F32),
            pltpu.VMEM((8, L), F32),
            pltpu.VMEM((4 * L, L), F32),
            pltpu.SemaphoreType.DMA((4,)),
            pltpu.SemaphoreType.DMA((len(STEPS),)),
        ],
        (
            in_hbm(tile_ids),
            in_hbm(offsets),
            in_hbm(tod.reshape(L, SAMP)),
            in_hbm(weights.reshape(L, SAMP)),
            in_hbm(pointing.reshape(L, SAMP, FOOT)),
        ),
        2**30,
        2**23,
        16,
    )
    got = exchange_rows(message)

    field, message, pick, place, shifts = whole_call(
        start_kernel,
        [WIDE, _shape((3, L, L), BF16), _shape((4, L, L), BF16), _shape((4, L, L), BF16), _shape((2, L, L), jnp.int32)],
        (got,),
    )
    got = exchange(message)

    message, foot, smooth = whole_call(
        first_apply_kernel,
        [_shape((2 * L, L), BF16), WIDE, WIDE],
        (got, get, put_2, shift, normal, field, neighbours),
        [pltpu.VMEM(MAP, F32)],
        2**28,
        2**22,
    )
    got = exchange_rows(message)

    image, message = whole_call(
        middle_kernel,
        [WIDE, _shape((3, L, L), BF16)],
        (got, field, smooth, pick, place, shifts),
    )
    got = exchange(message)

    message, residual, smooth, sums = whole_call(
        second_apply_kernel,
        [_shape((4 * L, L), BF16), WIDE, WIDE, _shape((1, L), F32)],
        (got, get, put_4, shift, normal, foot, field, image, smooth, neighbours),
        [pltpu.VMEM(MAP, F32)],
        2**28,
        2**22,
    )
    got = exchange_rows(message)

    return tuple(
        whole_call(
            last_kernel,
            [_shape((TILE, 8 * L), F32)] * 2,
            (got, place, shifts, field, image, residual, smooth, sums),
        )
    )


def solution(mesh):
    split = Mesh(mesh.devices.reshape(mesh.shape["det"], 4, 4, 2), DET_TM)
    in_specs = (
        P("det", TM, None),
        P("det", TM, None, None),
        P("det", TM, None),
        P("det", TM),
        P("det", TM),
        P(DET_TM, None),
    )
    out_specs = (P(DET_TM, None), P(DET_TM, None))
    return jax.shard_map(
        per_device, mesh=split, in_specs=in_specs, out_specs=out_specs, check_vma=False
    )
```

```python
import jax
import jax.numpy as jnp
from jax import lax
from jax.experimental import pallas as pl
from jax.experimental.pallas import tpu as pltpu
from jax.sharding import Mesh
from jax.sharding import PartitionSpec as P


DET_TM = ("det", "tm_0", "tm_1", "tm_2")
TM = ("tm_0", "tm_1", "tm_2")
SEND = ("tm_2", "tm_1", "tm_0", "det")
SAMP = 256
FOOT = 128
L = 128
TILE = 16
ROW_STEP = 16
SCALARS = 64

smooth_weight = 2.0
ridge_weight = 0.5

F32 = jnp.float32
BF16 = jnp.bfloat16


def _roll(x, shift, axis):
    return pltpu.roll(x, shift, axis)


def _iota(shape, dim):
    return lax.broadcasted_iota(jnp.int32, shape, dim)


def _dot(a, b):
    return jnp.dot(a, b, preferred_element_type=F32)


def _dot_nt(a, b):
    return lax.dot_general(a, b, (((1,), (1,)), ((), ())), preferred_element_type=F32)


def _onehot(mask):
    return jnp.where(mask, 1.0, 0.0).astype(BF16)


def _to_col(row):
    eye = _iota((L, L), 0) == _iota((L, L), 1)
    return jnp.sum(jnp.where(eye, row, 0.0), axis=1, keepdims=True)


def _to_row(col):
    eye = _iota((L, L), 0) == _iota((L, L), 1)
    return jnp.sum(jnp.where(eye, col, 0.0), axis=0, keepdims=True)


def _rotate(x, amount):
    step = 1
    for base in (8, 4, 4):
        digit = (amount >> (step.bit_length() - 1)) & (base - 1)
        turned = x
        for value in range(1, base):
            turned = jnp.where(digit == value, _roll(x, step * value, 1), turned)
        x = turned
        step *= base
    return x


def _as_row(ids, scratch):
    scratch[...] = jnp.zeros(scratch.shape, F32)
    scratch[0:2, 0:64] = ids.astype(F32)
    x = scratch[...]
    return x[0:1] + _roll(x, 64, 1)[1:2]


def _pieces(value, first):
    hi = value.astype(BF16).astype(F32)
    mid = (value - hi).astype(BF16).astype(F32)
    lo = value - hi - mid
    lane = _iota((1, L), 1)
    return jnp.where(
        lane == first, hi, jnp.where(lane == first + 1, mid, jnp.where(lane == first + 2, lo, 0.0))
    )


def _whole(row, first):
    lane = _iota((1, L), 1)
    return jnp.sum(
        jnp.where((lane >= first) & (lane < first + 3), row, 0.0), axis=1, keepdims=True
    )


def _total(x):
    return jnp.sum(jnp.sum(x, axis=0, keepdims=True), axis=1, keepdims=True)


def _owner(tile):
    det, tm_0, tm_1, tm_2 = tile >> 9, (tile >> 7) & 3, (tile >> 5) & 3, (tile >> 4) & 1
    return (tm_2 << 6) | (tm_1 << 4) | (tm_0 << 2) | det


def _blocks_of(owner_row, rows):
    line = _iota((L * rows, L), 0)
    return _onehot(line == owner_row * rows + (_iota((L * rows, L), 1) & 1))


def places(tile_row, offset_row):
    tile = tile_row.astype(jnp.int32)
    offset = offset_row.astype(jnp.int32)
    start_row = (offset >> 7) * ROW_STEP + (tile & 15)
    line = _iota((L, L), 0)
    place = 2 * (_iota((L, L), 1) & 1)
    facts = jnp.where(
        line == place,
        start_row.astype(F32),
        jnp.where(line == place + 1, (offset & 127).astype(F32), 0.0),
    ).astype(BF16)
    third = _onehot(_iota((4 * L, L), 0) == _owner(tile) * 4 + 2)
    return _dot_nt(third, facts)


def block_tables(tile_row, offset_row):
    owner = _owner(tile_row.astype(jnp.int32))
    shift = offset_row.astype(jnp.int32) & 127
    owner_col = _to_col(owner.astype(F32)).astype(jnp.int32)
    shift_col = _to_col(shift.astype(F32)).astype(jnp.int32)
    block = _iota((L, L), 0)
    device = _iota((L, L), 1)
    get = [_onehot((device == owner_col) & ((block & 1) == j)) for j in range(2)]
    return get, _blocks_of(owner, 2), _blocks_of(owner, 4), jnp.broadcast_to(shift_col, (L, L))


def owner_tables(facts):
    facts = facts.astype(F32)
    pick, place, shifts = [], [], []
    for j in range(2):
        start_col = facts[:, 2 * j : 2 * j + 1]
        start_row = _to_row(start_col)
        for step in (0, ROW_STEP):
            pick.append(_onehot(_iota((L, L), 1).astype(F32) == start_col + step))
            place.append(_onehot(_iota((L, L), 0).astype(F32) == start_row + step))
        shifts.append(jnp.broadcast_to(facts[:, 2 * j + 1 : 2 * j + 2], (L, L)).astype(jnp.int32))
    return pick, place, shifts


def add_up(got, place, shifts):
    lane = _iota((L, L), 1)
    total = None
    for j in range(2):
        x = got[j].astype(F32)
        upper = jnp.where(lane >= shifts[j], x, 0.0).astype(BF16)
        lower = jnp.where(lane < shifts[j], x, 0.0).astype(BF16)
        part = _dot(place[2 * j], upper) + _dot(place[2 * j + 1], lower)
        total = part if total is None else total + part
    return total


def reply(field, pick, shifts):
    lane = _iota((L, L), 1)
    field = field.astype(BF16)
    return [
        jnp.where(
            lane >= shifts[j], _dot(pick[2 * j], field), _dot(pick[2 * j + 1], field)
        ).astype(BF16)
        for j in range(2)
    ]


def edge_row(field):
    lane = _iota((TILE, L), 1)
    tile = _iota((TILE, L), 0)
    first = field[0:TILE, 0:1]
    last = field[L - TILE : L, L - 1 : L]
    out = jnp.zeros((TILE, L), F32)
    for k, value in enumerate((first, last)):
        hi = value.astype(BF16).astype(F32)
        out = out + jnp.where(lane == tile + 32 * k, hi, 0.0)
        out = out + jnp.where(lane == tile + 32 * k + 16, value - hi, 0.0)
    return jnp.sum(out, axis=0, keepdims=True)


def outer_edges(edges, neighbours):
    lane = _iota((TILE, L), 1)
    found = []
    for side, base in ((0, 32), (1, 0)):
        line = neighbours[side : side + 1].astype(F32)
        own = _iota((TILE, TILE), 0) == _iota((TILE, TILE), 1)
        tile = jnp.sum(jnp.where(own, line, 0.0), axis=1, keepdims=True).astype(jnp.int32)
        rows = _dot(_onehot(lane == _owner(tile)), edges)
        at = base + (tile & 15)
        found.append(
            jnp.sum(jnp.where((lane == at) | (lane == at + 16), rows, 0.0), axis=1, keepdims=True)
        )
    return found


def prior(field, before, after):
    lane = _iota((L, L), 1)
    to_right = _roll(field, 1, 1)
    to_left = _roll(field, L - 1, 1)
    edge = (TILE, L)
    left_in = jnp.concatenate([jnp.broadcast_to(before, edge), to_right[: L - TILE]], axis=0)
    right_in = jnp.concatenate([to_left[TILE:], jnp.broadcast_to(after, edge)], axis=0)
    lefts = jnp.where(lane == 0, left_in, to_right)
    rights = jnp.where(lane == L - 1, right_in, to_left)
    return smooth_weight * (2.0 * field - lefts - rights) + ridge_weight * field


def take_reply(got, get, shift):
    turned = _dot(get[0], got[0]) + _dot(get[1], got[1])
    return _rotate(turned.astype(BF16), ((L - shift) & 127).astype(jnp.int16)).astype(F32)


def send_back(back, put, shift):
    turned = _rotate(back.astype(BF16), shift.astype(jnp.int16))
    return _dot(put, turned)


CHUNK = 16
STEPS = (32, 48, 48)
DEPTH = 2


def rhs_kernel(
    tile_hbm, offset_hbm, tod_hbm, weight_hbm, beam_hbm,
    message_ref, normal_ref, get_ref, put_2_ref, put_4_ref, shift_ref,
    tile_ref, offset_ref, tod_ref, weight_ref, beam_ref, weighted, back, scratch, facts, small_sems, sems,
):
    small = [
        pltpu.make_async_copy(src, dst, small_sems.at[k])
        for k, (src, dst) in enumerate(
            (
                (tile_hbm, tile_ref),
                (offset_hbm, offset_ref),
                (tod_hbm, tod_ref),
                (weight_hbm, weight_ref),
            )
        )
    ]
    starts = [sum(STEPS[:k]) for k in range(len(STEPS))]
    beams = [
        pltpu.make_async_copy(
            beam_hbm.at[pl.ds(first, size)], beam_ref.at[pl.ds(first, size)], sems.at[k]
        )
        for k, (first, size) in enumerate(zip(starts, STEPS))
    ]

    for copy in small:
        copy.start()
    for copy in beams[:DEPTH]:
        copy.start()
    small[0].wait()
    small[1].wait()
    tile_row = _as_row(tile_ref[...], scratch)
    offset_row = _as_row(offset_ref[...], scratch)
    get, put_2, put_4, shift = block_tables(tile_row, offset_row)
    for j in range(2):
        get_ref[j] = get[j]
    put_2_ref[...] = put_2
    put_4_ref[...] = put_4
    shift_ref[...] = shift
    facts[...] = places(tile_row, offset_row)
    small[2].wait()
    small[3].wait()
    weighted[...] = (weight_ref[...] * tod_ref[...].astype(F32)).astype(BF16)
    row = _iota((CHUNK, FOOT), 0)

    for step, (start, size) in enumerate(zip(starts, STEPS)):
        beams[step].wait()
        if step + DEPTH < len(STEPS):
            beams[step + DEPTH].start()
        for first in range(start, start + size, CHUNK):
            rows = weighted[first : first + CHUNK]
            weight = weight_ref[first : first + CHUNK]
            out = jnp.zeros((CHUNK, FOOT), F32)
            for k in range(CHUNK):
                beam = beam_ref[first + k]
                turned = (beam.T.astype(F32) * weight[k : k + 1]).astype(BF16)
                found = _dot(jnp.concatenate([turned, rows], axis=0), beam)
                down, across = k % 2 * FOOT, k // 2 % 2 * FOOT
                normal_ref[(first + k) // 4, down : down + FOOT, across : across + FOOT] = found[
                    :FOOT
                ].astype(BF16)
                out = jnp.where(row == k, found[FOOT:], out)
            back[first : first + CHUNK] = out

    message_ref[...] = (facts[...] + send_back(back[...], put_4_ref[...], shift_ref[...])).astype(BF16)


def apply_normal(normal_ref, foot, back):
    row = _iota((CHUNK, FOOT), 0)
    for c in range(L // CHUNK):
        own = foot[c * CHUNK : (c + 1) * CHUNK]
        left = jnp.concatenate(
            [jnp.where((row & 1) == 0, own, 0.0), jnp.where((row & 1) == 1, own, 0.0)], axis=1
        ).astype(BF16)
        out = jnp.zeros((CHUNK, FOOT), F32)
        for q in range(CHUNK // 4):
            found = _dot(left, normal_ref[c * (CHUNK // 4) + q])
            out = jnp.where(
                (row >> 1) == 2 * q, found[:, :FOOT], jnp.where((row >> 1) == 2 * q + 1, found[:, FOOT:], out)
            )
        back[c * CHUNK : (c + 1) * CHUNK] = out
    return back[...]


def start_kernel(got_ref, field_ref, message_ref, pick_ref, place_ref, shift_ref):
    pick, place, shifts = owner_tables(got_ref[2])
    field = add_up((got_ref[0], got_ref[1]), place, shifts)
    replies = reply(field, pick, shifts)
    field_ref[...] = field
    message_ref[0] = replies[0]
    message_ref[1] = replies[1]
    message_ref[2] = jnp.broadcast_to(edge_row(field), (L, L)).astype(BF16)
    for k in range(4):
        pick_ref[k] = pick[k]
        place_ref[k] = place[k]
    for j in range(2):
        shift_ref[j] = shifts[j]


def first_apply_kernel(
    got_ref, get_ref, put_ref, shift_ref, normal_ref, field_ref, neighbour_ref, message_ref, foot_ref, prior_ref, back
):
    shift = shift_ref[...]
    foot = take_reply((got_ref[0], got_ref[1]), (get_ref[0], get_ref[1]), shift)
    foot_ref[...] = foot
    turned = apply_normal(normal_ref, foot, back)
    message_ref[...] = send_back(turned, put_ref[...], shift).astype(BF16)
    before, after = outer_edges(got_ref[2], neighbour_ref[...])
    prior_ref[...] = prior(field_ref[...], before, after)


def middle_kernel(got_ref, field_ref, smooth_ref, pick_ref, place_ref, shift_ref, image_ref, message_ref):
    field = field_ref[...]
    pick = [pick_ref[k] for k in range(4)]
    place = [place_ref[k] for k in range(4)]
    shifts = [shift_ref[j] for j in range(2)]
    image = add_up((got_ref[0], got_ref[1]), place, shifts) + smooth_ref[...]
    replies = reply(image, pick, shifts)
    image_ref[...] = image
    message_ref[0] = replies[0]
    message_ref[1] = replies[1]
    extra = (
        edge_row(image)
        + _pieces(_total(field * field), SCALARS)
        + _pieces(_total(field * image), SCALARS + 3)
    )
    message_ref[2] = jnp.broadcast_to(extra, (L, L)).astype(BF16)


def second_apply_kernel(
    got_ref, get_ref, put_ref, shift_ref, normal_ref, foot_ref, field_ref, image_ref, smooth_ref, neighbour_ref,
    message_ref, residual_ref, prior_ref, sums_ref, back,
):
    shift = shift_ref[...]
    sums = jnp.sum(got_ref[2].astype(F32), axis=0, keepdims=True)
    sums_ref[...] = sums
    step = _whole(sums, SCALARS) / _whole(sums, SCALARS + 3)
    taken = take_reply((got_ref[0], got_ref[1]), (get_ref[0], get_ref[1]), shift)
    foot = (foot_ref[...] - step * taken).astype(BF16).astype(F32)
    image = image_ref[...]
    before, after = outer_edges(got_ref[2], neighbour_ref[...])
    residual = field_ref[...] - step * image
    smooth = smooth_ref[...] - step * prior(image, before, after)
    residual_ref[...] = residual
    prior_ref[...] = smooth
    turned = apply_normal(normal_ref, foot, back)
    square = _total(residual * residual)
    product = _total(foot * turned + residual * smooth)
    extra = _pieces(square, SCALARS) + _pieces(product, SCALARS + 3)
    third = (_iota((4 * L, L), 0) & 3) == 2
    message_ref[...] = jnp.where(third, extra, send_back(turned, put_ref[...], shift)).astype(BF16)


def last_kernel(got_ref, place_ref, shift_ref, field_ref, image_ref, residual_ref, smooth_ref, sums_ref, solution_ref, rest_ref):
    place = [place_ref[k] for k in range(4)]
    shifts = [shift_ref[j] for j in range(2)]
    residual = residual_ref[...]
    field = field_ref[...]
    image = add_up((got_ref[0], got_ref[1]), place, shifts) + smooth_ref[...]
    sums = sums_ref[...]
    more = jnp.sum(got_ref[2].astype(F32), axis=0, keepdims=True)
    norm_first = _whole(sums, SCALARS)
    step_first = norm_first / _whole(sums, SCALARS + 3)
    norm = _whole(more, SCALARS)
    ratio = norm / norm_first
    step = norm / (_whole(more, SCALARS + 3) - ratio * (norm / step_first))
    solution = step_first * field + step * (residual + ratio * field)
    rest = residual - step * (image + ratio * image_ref[...])
    for q in range(8):
        solution_ref[:, q * L : (q + 1) * L] = solution[q * TILE : (q + 1) * TILE]
        rest_ref[:, q * L : (q + 1) * L] = rest[q * TILE : (q + 1) * TILE]


def _shape(shape, dtype):
    return jax.ShapeDtypeStruct(shape, dtype)


def _full(shape):
    return pl.BlockSpec(shape, lambda g: (0,) * len(shape))


MAP = (L, L)
WIDE = _shape(MAP, F32)


def call(kernel, grid, in_specs, outs, out_specs, scratch, args, flops, size, vmem):
    return pl.pallas_call(
        kernel,
        grid=grid,
        in_specs=in_specs,
        out_specs=out_specs,
        out_shape=outs,
        scratch_shapes=scratch,
        compiler_params=pltpu.CompilerParams(vmem_limit_bytes=vmem * 2**20),
        cost_estimate=pl.CostEstimate(flops=flops, bytes_accessed=size, transcendentals=0),
    )(*args)


def whole_call(kernel, outs, args, scratch=(), flops=2**25, size=2**19):
    vmem = pl.BlockSpec(memory_space=pltpu.VMEM)
    return call(
        kernel, (), [vmem] * len(args), outs, [vmem] * len(outs), scratch, args, flops, size, 8
    )


def in_hbm(x):
    return pltpu.with_memory_space_constraint(x, pltpu.HBM)


def exchange(x):
    return lax.all_to_all(x, SEND, split_axis=1, concat_axis=1, tiled=True)


def exchange_rows(x):
    x = lax.all_to_all(x.reshape(L, -1, L), SEND, split_axis=0, concat_axis=0, tiled=True)
    return x.transpose(1, 0, 2)


def per_device(tod, pointing, weights, tile_ids, offsets, neighbours):
    neighbours = neighbours.T

    message, normal, get, put_2, put_4, shift = call(
        rhs_kernel,
        (),
        [pl.BlockSpec(memory_space=pltpu.HBM)] * 5,
        [
            _shape((4 * L, L), BF16),
            pltpu.VMEM((L // 4, 2 * FOOT, 2 * FOOT), BF16),
            _shape((2, L, L), BF16),
            _shape((2 * L, L), BF16),
            _shape((4 * L, L), BF16),
            _shape((L, L), jnp.int32),
        ],
        [pl.BlockSpec(memory_space=pltpu.VMEM)] * 6,
        [
            pltpu.VMEM(tile_ids.shape, jnp.int32),
            pltpu.VMEM(offsets.shape, jnp.int32),
            pltpu.VMEM((L, SAMP), BF16),
            pltpu.VMEM((L, SAMP), F32),
            pltpu.VMEM((L, SAMP, FOOT), BF16),
            pltpu.VMEM((L, SAMP), BF16),
            pltpu.VMEM((L, FOOT), F32),
            pltpu.VMEM((8, L), F32),
            pltpu.VMEM((4 * L, L), F32),
            pltpu.SemaphoreType.DMA((4,)),
            pltpu.SemaphoreType.DMA((len(STEPS),)),
        ],
        (
            in_hbm(tile_ids),
            in_hbm(offsets),
            in_hbm(tod.reshape(L, SAMP)),
            in_hbm(weights.reshape(L, SAMP)),
            in_hbm(pointing.reshape(L, SAMP, FOOT)),
        ),
        2**30,
        2**23,
        16,
    )
    got = exchange_rows(message)

    field, message, pick, place, shifts = whole_call(
        start_kernel,
        [WIDE, _shape((3, L, L), BF16), _shape((4, L, L), BF16), _shape((4, L, L), BF16), _shape((2, L, L), jnp.int32)],
        (got,),
    )
    got = exchange(message)

    message, foot, smooth = whole_call(
        first_apply_kernel,
        [_shape((2 * L, L), BF16), WIDE, WIDE],
        (got, get, put_2, shift, normal, field, neighbours),
        [pltpu.VMEM(MAP, F32)],
        2**28,
        2**22,
    )
    got = exchange_rows(message)

    image, message = whole_call(
        middle_kernel,
        [WIDE, _shape((3, L, L), BF16)],
        (got, field, smooth, pick, place, shifts),
    )
    got = exchange(message)

    message, residual, smooth, sums = whole_call(
        second_apply_kernel,
        [_shape((4 * L, L), BF16), WIDE, WIDE, _shape((1, L), F32)],
        (got, get, put_4, shift, normal, foot, field, image, smooth, neighbours),
        [pltpu.VMEM(MAP, F32)],
        2**28,
        2**22,
    )
    got = exchange_rows(message)

    return tuple(
        whole_call(
            last_kernel,
            [_shape((TILE, 8 * L), F32)] * 2,
            (got, place, shifts, field, image, residual, smooth, sums),
        )
    )


def solution(mesh):
    split = Mesh(mesh.devices.reshape(mesh.shape["det"], 4, 4, 2), DET_TM)
    in_specs = (
        P("det", TM, None),
        P("det", TM, None, None),
        P("det", TM, None),
        P("det", TM),
        P("det", TM),
        P(DET_TM, None),
    )
    out_specs = (P(DET_TM, None), P(DET_TM, None))
    return jax.shard_map(
        per_device, mesh=split, in_specs=in_specs, out_specs=out_specs, check_vma=False
    )
```

```python
import jax
import jax.numpy as jnp
from jax import lax
from jax.experimental import pallas as pl
from jax.experimental.pallas import tpu as pltpu
from jax.sharding import Mesh
from jax.sharding import PartitionSpec as P


DET_TM = ("det", "tm_0", "tm_1", "tm_2")
TM = ("tm_0", "tm_1", "tm_2")
SEND = ("tm_2", "tm_1", "tm_0", "det")
SAMP = 256
FOOT = 128
L = 128
TILE = 16
ROW_STEP = 16
SCALARS = 64

smooth_weight = 2.0
ridge_weight = 0.5

F32 = jnp.float32
BF16 = jnp.bfloat16


def _roll(x, shift, axis):
    return pltpu.roll(x, shift, axis)


def _iota(shape, dim):
    return lax.broadcasted_iota(jnp.int32, shape, dim)


def _dot(a, b):
    return jnp.dot(a, b, preferred_element_type=F32)


def _dot_nt(a, b):
    return lax.dot_general(a, b, (((1,), (1,)), ((), ())), preferred_element_type=F32)


def _onehot(mask):
    return jnp.where(mask, 1.0, 0.0).astype(BF16)


def _to_col(row):
    eye = _iota((L, L), 0) == _iota((L, L), 1)
    return jnp.sum(jnp.where(eye, row, 0.0), axis=1, keepdims=True)


def _to_row(col):
    eye = _iota((L, L), 0) == _iota((L, L), 1)
    return jnp.sum(jnp.where(eye, col, 0.0), axis=0, keepdims=True)


def _rotate(x, amount):
    step = 1
    for base in (8, 4, 4):
        digit = (amount >> (step.bit_length() - 1)) & (base - 1)
        turned = x
        for value in range(1, base):
            turned = jnp.where(digit == value, _roll(x, step * value, 1), turned)
        x = turned
        step *= base
    return x


def _as_row(ids, scratch):
    scratch[...] = jnp.zeros(scratch.shape, F32)
    scratch[0:2, 0:64] = ids.astype(F32)
    x = scratch[...]
    return x[0:1] + _roll(x, 64, 1)[1:2]


def _pieces(value, first):
    hi = value.astype(BF16).astype(F32)
    mid = (value - hi).astype(BF16).astype(F32)
    lo = value - hi - mid
    lane = _iota((1, L), 1)
    return jnp.where(
        lane == first, hi, jnp.where(lane == first + 1, mid, jnp.where(lane == first + 2, lo, 0.0))
    )


def _whole(row, first):
    lane = _iota((1, L), 1)
    return jnp.sum(
        jnp.where((lane >= first) & (lane < first + 3), row, 0.0), axis=1, keepdims=True
    )


def _total(x):
    return jnp.sum(jnp.sum(x, axis=0, keepdims=True), axis=1, keepdims=True)


def _owner(tile):
    det, tm_0, tm_1, tm_2 = tile >> 9, (tile >> 7) & 3, (tile >> 5) & 3, (tile >> 4) & 1
    return (tm_2 << 6) | (tm_1 << 4) | (tm_0 << 2) | det


def _blocks_of(owner_row, rows):
    line = _iota((L * rows, L), 0)
    return _onehot(line == owner_row * rows + (_iota((L * rows, L), 1) & 1))


def places(tile_row, offset_row):
    tile = tile_row.astype(jnp.int32)
    offset = offset_row.astype(jnp.int32)
    start_row = (offset >> 7) * ROW_STEP + (tile & 15)
    line = _iota((L, L), 0)
    place = 2 * (_iota((L, L), 1) & 1)
    facts = jnp.where(
        line == place,
        start_row.astype(F32),
        jnp.where(line == place + 1, (offset & 127).astype(F32), 0.0),
    ).astype(BF16)
    third = _onehot(_iota((4 * L, L), 0) == _owner(tile) * 4 + 2)
    return _dot_nt(third, facts)


def block_tables(tile_row, offset_row):
    owner = _owner(tile_row.astype(jnp.int32))
    shift = offset_row.astype(jnp.int32) & 127
    owner_col = _to_col(owner.astype(F32)).astype(jnp.int32)
    shift_col = _to_col(shift.astype(F32)).astype(jnp.int32)
    block = _iota((L, L), 0)
    device = _iota((L, L), 1)
    get = [_onehot((device == owner_col) & ((block & 1) == j)) for j in range(2)]
    return get, _blocks_of(owner, 2), _blocks_of(owner, 4), jnp.broadcast_to(shift_col, (L, L))


def owner_tables(facts):
    facts = facts.astype(F32)
    pick, place, shifts = [], [], []
    for j in range(2):
        start_col = facts[:, 2 * j : 2 * j + 1]
        start_row = _to_row(start_col)
        for step in (0, ROW_STEP):
            pick.append(_onehot(_iota((L, L), 1).astype(F32) == start_col + step))
            place.append(_onehot(_iota((L, L), 0).astype(F32) == start_row + step))
        shifts.append(jnp.broadcast_to(facts[:, 2 * j + 1 : 2 * j + 2], (L, L)).astype(jnp.int32))
    return jnp.concatenate(pick, axis=0), jnp.concatenate(place, axis=1), shifts


def add_up(got, place, shifts):
    lane = _iota((L, L), 1)
    parts = []
    for j in range(2):
        x = got[j].astype(F32)
        parts.append(jnp.where(lane >= shifts[j], x, 0.0).astype(BF16))
        parts.append(jnp.where(lane < shifts[j], x, 0.0).astype(BF16))
    return _dot(place, jnp.concatenate(parts, axis=0))


def reply(field, pick, shifts):
    lane = _iota((L, L), 1)
    found = _dot(pick, field.astype(BF16))
    return [
        jnp.where(
            lane >= shifts[j],
            found[2 * j * L : (2 * j + 1) * L],
            found[(2 * j + 1) * L : (2 * j + 2) * L],
        ).astype(BF16)
        for j in range(2)
    ]


def edge_row(field):
    lane = _iota((TILE, L), 1)
    tile = _iota((TILE, L), 0)
    first = field[0:TILE, 0:1]
    last = field[L - TILE : L, L - 1 : L]
    out = jnp.zeros((TILE, L), F32)
    for k, value in enumerate((first, last)):
        hi = value.astype(BF16).astype(F32)
        out = out + jnp.where(lane == tile + 32 * k, hi, 0.0)
        out = out + jnp.where(lane == tile + 32 * k + 16, value - hi, 0.0)
    return jnp.sum(out, axis=0, keepdims=True)


def outer_edges(edges, neighbours):
    lane = _iota((TILE, L), 1)
    found = []
    for side, base in ((0, 32), (1, 0)):
        line = neighbours[side : side + 1].astype(F32)
        own = _iota((TILE, TILE), 0) == _iota((TILE, TILE), 1)
        tile = jnp.sum(jnp.where(own, line, 0.0), axis=1, keepdims=True).astype(jnp.int32)
        rows = _dot(_onehot(lane == _owner(tile)), edges)
        at = base + (tile & 15)
        found.append(
            jnp.sum(jnp.where((lane == at) | (lane == at + 16), rows, 0.0), axis=1, keepdims=True)
        )
    return found


def prior(field, before, after):
    lane = _iota((L, L), 1)
    to_right = _roll(field, 1, 1)
    to_left = _roll(field, L - 1, 1)
    edge = (TILE, L)
    left_in = jnp.concatenate([jnp.broadcast_to(before, edge), to_right[: L - TILE]], axis=0)
    right_in = jnp.concatenate([to_left[TILE:], jnp.broadcast_to(after, edge)], axis=0)
    lefts = jnp.where(lane == 0, left_in, to_right)
    rights = jnp.where(lane == L - 1, right_in, to_left)
    return smooth_weight * (2.0 * field - lefts - rights) + ridge_weight * field


def take_reply(got, get, shift):
    turned = _dot(get, jnp.concatenate(got, axis=0))
    return _rotate(turned.astype(BF16), ((L - shift) & 127).astype(jnp.int16)).astype(F32)


def send_back(back, put, shift):
    turned = _rotate(back.astype(BF16), shift.astype(jnp.int16))
    return _dot(put, turned)


CHUNK = 16
STEPS = (32, 48, 48)
DEPTH = 2


def rhs_kernel(
    tile_hbm, offset_hbm, tod_hbm, weight_hbm, beam_hbm,
    message_ref, normal_ref, get_ref, put_2_ref, put_4_ref, shift_ref,
    tile_ref, offset_ref, tod_ref, weight_ref, beam_ref, weighted, back, scratch, facts, small_sems, sems,
):
    small = [
        pltpu.make_async_copy(src, dst, small_sems.at[k])
        for k, (src, dst) in enumerate(
            (
                (tile_hbm, tile_ref),
                (offset_hbm, offset_ref),
                (tod_hbm, tod_ref),
                (weight_hbm, weight_ref),
            )
        )
    ]
    starts = [sum(STEPS[:k]) for k in range(len(STEPS))]
    beams = [
        pltpu.make_async_copy(
            beam_hbm.at[pl.ds(first, size)], beam_ref.at[pl.ds(first, size)], sems.at[k]
        )
        for k, (first, size) in enumerate(zip(starts, STEPS))
    ]

    for copy in small:
        copy.start()
    for copy in beams[:DEPTH]:
        copy.start()
    small[0].wait()
    small[1].wait()
    tile_row = _as_row(tile_ref[...], scratch)
    offset_row = _as_row(offset_ref[...], scratch)
    get, put_2, put_4, shift = block_tables(tile_row, offset_row)
    get_ref[...] = jnp.concatenate(get, axis=1)
    put_2_ref[...] = put_2
    put_4_ref[...] = put_4
    shift_ref[...] = shift
    facts[...] = places(tile_row, offset_row)
    small[2].wait()
    small[3].wait()
    weighted[...] = (weight_ref[...] * tod_ref[...].astype(F32)).astype(BF16)
    row = _iota((CHUNK, FOOT), 0)

    for step, (start, size) in enumerate(zip(starts, STEPS)):
        beams[step].wait()
        if step + DEPTH < len(STEPS):
            beams[step + DEPTH].start()
        for first in range(start, start + size, CHUNK):
            rows = weighted[first : first + CHUNK]
            weight = weight_ref[first : first + CHUNK]
            out = jnp.zeros((CHUNK, FOOT), F32)
            for k in range(CHUNK):
                beam = beam_ref[first + k]
                turned = (beam.T.astype(F32) * weight[k : k + 1]).astype(BF16)
                found = _dot(jnp.concatenate([turned, rows], axis=0), beam)
                down, across = k % 2 * FOOT, k // 2 % 2 * FOOT
                normal_ref[(first + k) // 4, down : down + FOOT, across : across + FOOT] = found[
                    :FOOT
                ].astype(BF16)
                out = jnp.where(row == k, found[FOOT:], out)
            back[first : first + CHUNK] = out

    message_ref[...] = (facts[...] + send_back(back[...], put_4_ref[...], shift_ref[...])).astype(BF16)


def apply_normal(normal_ref, foot, back):
    row = _iota((CHUNK, FOOT), 0)
    for c in range(L // CHUNK):
        own = foot[c * CHUNK : (c + 1) * CHUNK]
        left = jnp.concatenate(
            [jnp.where((row & 1) == 0, own, 0.0), jnp.where((row & 1) == 1, own, 0.0)], axis=1
        ).astype(BF16)
        out = jnp.zeros((CHUNK, FOOT), F32)
        for q in range(CHUNK // 4):
            found = _dot(left, normal_ref[c * (CHUNK // 4) + q])
            out = jnp.where(
                (row >> 1) == 2 * q, found[:, :FOOT], jnp.where((row >> 1) == 2 * q + 1, found[:, FOOT:], out)
            )
        back[c * CHUNK : (c + 1) * CHUNK] = out
    return back[...]


def start_kernel(got_ref, field_ref, message_ref, pick_ref, place_ref, shift_ref):
    pick, place, shifts = owner_tables(got_ref[2])
    field = add_up((got_ref[0], got_ref[1]), place, shifts)
    replies = reply(field, pick, shifts)
    field_ref[...] = field
    message_ref[0] = replies[0]
    message_ref[1] = replies[1]
    message_ref[2] = jnp.broadcast_to(edge_row(field), (L, L)).astype(BF16)
    pick_ref[...] = pick
    place_ref[...] = place
    for j in range(2):
        shift_ref[j] = shifts[j]


def first_apply_kernel(
    got_ref, get_ref, put_ref, shift_ref, normal_ref, field_ref, neighbour_ref, message_ref, foot_ref, prior_ref, back
):
    shift = shift_ref[...]
    foot = take_reply((got_ref[0], got_ref[1]), get_ref[...], shift)
    foot_ref[...] = foot
    turned = apply_normal(normal_ref, foot, back)
    message_ref[...] = send_back(turned, put_ref[...], shift).astype(BF16)
    before, after = outer_edges(got_ref[2], neighbour_ref[...])
    prior_ref[...] = prior(field_ref[...], before, after)


def middle_kernel(got_ref, field_ref, smooth_ref, pick_ref, place_ref, shift_ref, image_ref, message_ref):
    field = field_ref[...]
    pick = pick_ref[...]
    place = place_ref[...]
    shifts = [shift_ref[j] for j in range(2)]
    image = add_up((got_ref[0], got_ref[1]), place, shifts) + smooth_ref[...]
    replies = reply(image, pick, shifts)
    image_ref[...] = image
    message_ref[0] = replies[0]
    message_ref[1] = replies[1]
    extra = (
        edge_row(image)
        + _pieces(_total(field * field), SCALARS)
        + _pieces(_total(field * image), SCALARS + 3)
    )
    message_ref[2] = jnp.broadcast_to(extra, (L, L)).astype(BF16)


def second_apply_kernel(
    got_ref, get_ref, put_ref, shift_ref, normal_ref, foot_ref, field_ref, image_ref, smooth_ref, neighbour_ref,
    message_ref, residual_ref, prior_ref, sums_ref, back,
):
    shift = shift_ref[...]
    sums = jnp.sum(got_ref[2].astype(F32), axis=0, keepdims=True)
    sums_ref[...] = sums
    step = _whole(sums, SCALARS) / _whole(sums, SCALARS + 3)
    taken = take_reply((got_ref[0], got_ref[1]), get_ref[...], shift)
    foot = (foot_ref[...] - step * taken).astype(BF16).astype(F32)
    image = image_ref[...]
    before, after = outer_edges(got_ref[2], neighbour_ref[...])
    residual = field_ref[...] - step * image
    smooth = smooth_ref[...] - step * prior(image, before, after)
    residual_ref[...] = residual
    prior_ref[...] = smooth
    turned = apply_normal(normal_ref, foot, back)
    square = _total(residual * residual)
    product = _total(foot * turned + residual * smooth)
    extra = _pieces(square, SCALARS) + _pieces(product, SCALARS + 3)
    third = (_iota((4 * L, L), 0) & 3) == 2
    message_ref[...] = jnp.where(third, extra, send_back(turned, put_ref[...], shift)).astype(BF16)


def last_kernel(got_ref, place_ref, shift_ref, field_ref, image_ref, residual_ref, smooth_ref, sums_ref, solution_ref, rest_ref):
    place = place_ref[...]
    shifts = [shift_ref[j] for j in range(2)]
    residual = residual_ref[...]
    field = field_ref[...]
    image = add_up((got_ref[0], got_ref[1]), place, shifts) + smooth_ref[...]
    sums = sums_ref[...]
    more = jnp.sum(got_ref[2].astype(F32), axis=0, keepdims=True)
    norm_first = _whole(sums, SCALARS)
    step_first = norm_first / _whole(sums, SCALARS + 3)
    norm = _whole(more, SCALARS)
    ratio = norm / norm_first
    step = norm / (_whole(more, SCALARS + 3) - ratio * (norm / step_first))
    solution = step_first * field + step * (residual + ratio * field)
    rest = residual - step * (image + ratio * image_ref[...])
    for q in range(8):
        solution_ref[:, q * L : (q + 1) * L] = solution[q * TILE : (q + 1) * TILE]
        rest_ref[:, q * L : (q + 1) * L] = rest[q * TILE : (q + 1) * TILE]


def _shape(shape, dtype):
    return jax.ShapeDtypeStruct(shape, dtype)


def _full(shape):
    return pl.BlockSpec(shape, lambda g: (0,) * len(shape))


MAP = (L, L)
WIDE = _shape(MAP, F32)


def call(kernel, grid, in_specs, outs, out_specs, scratch, args, flops, size, vmem):
    return pl.pallas_call(
        kernel,
        grid=grid,
        in_specs=in_specs,
        out_specs=out_specs,
        out_shape=outs,
        scratch_shapes=scratch,
        compiler_params=pltpu.CompilerParams(vmem_limit_bytes=vmem * 2**20),
        cost_estimate=pl.CostEstimate(flops=flops, bytes_accessed=size, transcendentals=0),
    )(*args)


def whole_call(kernel, outs, args, scratch=(), flops=2**25, size=2**19):
    vmem = pl.BlockSpec(memory_space=pltpu.VMEM)
    return call(
        kernel, (), [vmem] * len(args), outs, [vmem] * len(outs), scratch, args, flops, size, 8
    )


def in_hbm(x):
    return pltpu.with_memory_space_constraint(x, pltpu.HBM)


def exchange(x):
    return lax.all_to_all(x, SEND, split_axis=1, concat_axis=1, tiled=True)


def exchange_rows(x):
    x = lax.all_to_all(x.reshape(L, -1, L), SEND, split_axis=0, concat_axis=0, tiled=True)
    return x.transpose(1, 0, 2)


def per_device(tod, pointing, weights, tile_ids, offsets, neighbours):
    neighbours = neighbours.T

    message, normal, get, put_2, put_4, shift = call(
        rhs_kernel,
        (),
        [pl.BlockSpec(memory_space=pltpu.HBM)] * 5,
        [
            _shape((4 * L, L), BF16),
            pltpu.VMEM((L // 4, 2 * FOOT, 2 * FOOT), BF16),
            _shape((L, 2 * L), BF16),
            _shape((2 * L, L), BF16),
            _shape((4 * L, L), BF16),
            _shape((L, L), jnp.int32),
        ],
        [pl.BlockSpec(memory_space=pltpu.VMEM)] * 6,
        [
            pltpu.VMEM(tile_ids.shape, jnp.int32),
            pltpu.VMEM(offsets.shape, jnp.int32),
            pltpu.VMEM((L, SAMP), BF16),
            pltpu.VMEM((L, SAMP), F32),
            pltpu.VMEM((L, SAMP, FOOT), BF16),
            pltpu.VMEM((L, SAMP), BF16),
            pltpu.VMEM((L, FOOT), F32),
            pltpu.VMEM((8, L), F32),
            pltpu.VMEM((4 * L, L), F32),
            pltpu.SemaphoreType.DMA((4,)),
            pltpu.SemaphoreType.DMA((len(STEPS),)),
        ],
        (
            in_hbm(tile_ids),
            in_hbm(offsets),
            in_hbm(tod.reshape(L, SAMP)),
            in_hbm(weights.reshape(L, SAMP)),
            in_hbm(pointing.reshape(L, SAMP, FOOT)),
        ),
        2**30,
        2**23,
        16,
    )
    got = exchange_rows(message)

    field, message, pick, place, shifts = whole_call(
        start_kernel,
        [WIDE, _shape((3, L, L), BF16), _shape((4 * L, L), BF16), _shape((L, 4 * L), BF16), _shape((2, L, L), jnp.int32)],
        (got,),
    )
    got = exchange(message)

    message, foot, smooth = whole_call(
        first_apply_kernel,
        [_shape((2 * L, L), BF16), WIDE, WIDE],
        (got, get, put_2, shift, normal, field, neighbours),
        [pltpu.VMEM(MAP, F32)],
        2**28,
        2**22,
    )
    got = exchange_rows(message)

    image, message = whole_call(
        middle_kernel,
        [WIDE, _shape((3, L, L), BF16)],
        (got, field, smooth, pick, place, shifts),
    )
    got = exchange(message)

    message, residual, smooth, sums = whole_call(
        second_apply_kernel,
        [_shape((4 * L, L), BF16), WIDE, WIDE, _shape((1, L), F32)],
        (got, get, put_4, shift, normal, foot, field, image, smooth, neighbours),
        [pltpu.VMEM(MAP, F32)],
        2**28,
        2**22,
    )
    got = exchange_rows(message)

    return tuple(
        whole_call(
            last_kernel,
            [_shape((TILE, 8 * L), F32)] * 2,
            (got, place, shifts, field, image, residual, smooth, sums),
        )
    )


def solution(mesh):
    split = Mesh(mesh.devices.reshape(mesh.shape["det"], 4, 4, 2), DET_TM)
    in_specs = (
        P("det", TM, None),
        P("det", TM, None, None),
        P("det", TM, None),
        P("det", TM),
        P("det", TM),
        P(DET_TM, None),
    )
    out_specs = (P(DET_TM, None), P(DET_TM, None))
    return jax.shard_map(
        per_device, mesh=split, in_specs=in_specs, out_specs=out_specs, check_vma=False
    )
```
